32 devices in a mesh: frames: 2 (over x), lenslet: 16 (over z, y, core).
Axes of the slice: x: 2, y: 2, z: 4, core: 2. Of those that a mesh axis runs over, the one named last changes fastest.
Arguments:
- volume: bfloat16 [8, 256, 64, 400], P('frames', 'lenslet'), parts along dimension 0, may hold values from 0.099609375 to 1
- measured: float32 [512, 64, 400], P(('frames', 'lenslet')), parts along dimension 0, may hold values from 0.2 to 2
- operator_rows: bfloat16 [12800, 400], P('lenslet'), may hold values from 2.9831426e-10 to 0.0029907227
- offset_counts: int32 [4], replicated, may hold values from 1 to 25, 32 in all
- offset_table: int32 [32, 2], replicated, may hold values from -2 to 2
- dark_level: float32 [400], replicated, may hold values from 0.2 to 1
Outputs:
- predicted: float32 [512, 64, 400], P(('frames', 'lenslet')), parts along dimension 0
- ratio: float32 [512, 64, 400], P(('frames', 'lenslet')), parts along dimension 0
The draws below stay inside these ranges and needn't reach their ends.
There are 2 independent parts, one for each index of `frames`. The reference program is written for one: setup_inputs(seed, part) draws one part's arguments, and reference() takes and returns one part's arrays. A program takes and returns all parts, laid end to end along the dimension named above; an argument that names none is the same for every part. Nothing has to cross between parts.
Inputs may be any that keep to these rules, and one draw needn't show every extreme that they name: `offset_counts`: counts sum to 32.
All inputs are finite; a program needn't handle non-finite values.
Results may differ from the reference program's by a relative error of at most 0.0003.
Values may be sent and summed in bfloat16 or wider, within the bound.
No kernel may reach another device: no remote copies, remote signals or barrier semaphores. Data moves between devices by JAX's collectives and lax.ppermute only.
A program may use at most 192 MiB of HBM per device.

```python
import math
import jax
import jax.numpy as jnp
import numpy as np
from jax import lax

PIX = 400
LX = 64
DEPTHS = 4
NOPS = 32
MOST_OFFSETS = 25
REACH = 2
ROWS = 256


def place_ends(values, own_key, least, high):
    spot = [jax.random.randint(jax.random.fold_in(own_key, axis), (), 0, length) for axis, length in enumerate(values.shape)]
    longest = values.shape.index(max(values.shape))
    beside = spot[:longest] + [(spot[longest] + 1) % values.shape[longest]] + spot[longest + 1:]
    return values.at[tuple(spot)].set(least).at[tuple(beside)].set(high)


def levels(own_key, dims, pieces, least, high):
    def one(position, parts):
        draws = jax.random.uniform(jax.random.fold_in(jax.random.fold_in(own_key, 6), position), (parts,), jnp.float32, least / len(pieces), high / len(pieces))
        return jnp.repeat(jnp.exp(draws), dims[position] // parts).reshape((-1,) + (1,) * (len(dims) - position - 1))

    loudness = one(*pieces[0])
    for cut in pieces[1:]:
        loudness = loudness * one(*cut)
    return loudness


def length_profile(count, total, limit, skew):
    loads = [(1 << 20) // math.isqrt(grade ** skew) + 1 for grade in range(2, count + 1)]
    surplus, given = total - limit - (count - 1), [1] * (count - 1)
    while surplus > 0:
        candidates = [i for i in range(count - 1) if given[i] < limit]
        whole, left = sum([loads[i] for i in candidates]), surplus
        for i in candidates:
            addition = min(limit - given[i], max(1, left * loads[i] // whole), surplus)
            given[i] = given[i] + addition
            surplus = surplus - addition
    return np.array([limit] + given)


def ragged_sizes(rng, count, total, reach, slope):
    if count == 2:
        one = jax.random.randint(rng, (), max(1, total - reach), min(reach, total - 1) + 1)
        return jnp.stack([one, total - one])
    sizes = jnp.asarray(length_profile(count, total, reach, slope), jnp.int32)
    twos = (count - 1) // 2
    giver, taker = sizes[1:1 + 2 * twos:2], sizes[2:2 + 2 * twos:2]
    margin = jnp.minimum(giver - 1, reach - taker)
    shifted = jax.random.randint(jax.random.fold_in(rng, 1), (twos,), 0, 1 << 20) % (margin + 1)
    sizes = sizes.at[1:1 + 2 * twos:2].set(giver - shifted).at[2:2 + 2 * twos:2].set(taker + shifted)
    return sizes[jax.random.permutation(jax.random.fold_in(rng, 2), count)]


def setup_inputs(seed: int = 0, part: int = 0) -> dict:
    key_list = jax.random.split(jax.random.key(seed), 7)
    part_keys = jax.random.split(jax.random.fold_in(key_list[6], part), 7)
    volume = jnp.clip(jnp.exp(math.log(1.0) - 2.306499 * jax.random.uniform(part_keys[0], (DEPTHS, ROWS, LX, PIX), jnp.float32) ** levels(part_keys[0], (DEPTHS, ROWS, LX, PIX), ((1, 16),), -0.2, 0.2)), 0.099609375, 1.0).astype(jnp.bfloat16)
    measured = jnp.clip(jnp.exp(math.log(2.0) - 2.3025851 * jax.random.uniform(part_keys[1], (ROWS, LX, PIX), jnp.float32) ** levels(part_keys[1], (ROWS, LX, PIX), ((0, 16),), -0.2, 0.2)), 0.2, 2.0)
    operator_rows = jnp.clip(jnp.exp(math.log(0.0029907227) - 16.1206334 * jax.random.uniform(key_list[2], (NOPS * PIX, PIX), jnp.float32) ** levels(key_list[2], (NOPS * PIX, PIX), ((0, 16),), -0.2, 0.2)), 2.9831426218152046e-10, 0.0029907227).astype(jnp.bfloat16)
    offset_counts = ragged_sizes(key_list[3], DEPTHS, NOPS, MOST_OFFSETS, 0).astype(jnp.int32)
    offset_table = place_ends(jax.random.randint(key_list[4], (NOPS, 2), -2, 3), jax.random.fold_in(key_list[4], 1), -2, 2).astype(jnp.int32)
    dark_level = jnp.clip(jnp.exp(jax.random.uniform(key_list[5], (PIX,), jnp.float32, math.log(0.2), math.log(1.0))), 0.2, 1.0)
    return {"volume": volume, "measured": measured, "operator_rows": operator_rows, "offset_counts": offset_counts, "offset_table": offset_table, "dark_level": dark_level}


def reference(volume, measured, operator_rows, offset_counts, offset_table, dark_level):
    padded = jnp.pad(volume, ((0, 0), (REACH, REACH), (REACH, REACH), (0, 0)))
    ends = jnp.cumsum(offset_counts).astype(jnp.int32)
    positions = jnp.arange(NOPS, dtype=jnp.int32)
    depth_of = jnp.sum((positions[:, None] >= ends[None, :]).astype(jnp.int32), axis=1).astype(jnp.int32)

    def accumulate(index, total):
        index = jnp.asarray(index).astype(jnp.int32)
        start_row = (offset_table[index, 0] + REACH).astype(jnp.int32)
        start_col = (offset_table[index, 1] + REACH).astype(jnp.int32)
        slab = lax.dynamic_slice(padded, (depth_of[index], start_row, start_col, jnp.int32(0)), (1, ROWS, LX, PIX))
        slab = slab.reshape(ROWS * LX, PIX)
        block = lax.dynamic_slice_in_dim(operator_rows, (index * PIX).astype(jnp.int32), PIX, 0)
        return total + jnp.dot(slab, block, preferred_element_type=jnp.float32)

    total = lax.fori_loop(0, NOPS, accumulate, jnp.zeros((ROWS * LX, PIX), jnp.float32))
    predicted = total.reshape(ROWS, LX, PIX)
    ratio = measured / (predicted + dark_level)
    return (predicted, ratio)
```

```python
import jax
import jax.numpy as jnp
from jax import lax
from jax.experimental import pallas as pl
from jax.experimental.pallas import tpu as pltpu
from jax.sharding import PartitionSpec as P

REACH = 2
SHIFTS = 2 * REACH + 1
VMEM = 60 * 1024 * 1024


def passed_along(block, axis, distance):
    devices = range(lax.axis_size(axis))
    route = [(i - distance, i) for i in devices if i - distance in devices]
    return lax.ppermute(block, axis, route)


def shift_kernel(own_ref, above_ref, below_ref, out_ref):
    rows, columns, pixels = own_ref.shape[1:]
    col = lax.broadcasted_iota(jnp.int32, (columns, pixels), 0)

    def put(row, plane):
        wide = plane.astype(jnp.float32)
        for s in range(SHIFTS):
            step = s - REACH
            if step == 0:
                moved = wide
            else:
                moved = pltpu.roll(wide, (-step) % columns, 0)
                inside = col < columns - step if step > 0 else col >= -step
                moved = jnp.where(inside, moved, 0.0)
            out_ref[s, 0, row] = moved.astype(jnp.bfloat16)

    for r in range(REACH):
        put(r, above_ref[0, r])
        put(rows + REACH + r, below_ref[0, r])

    def step(r, carry):
        put(r + REACH, own_ref[0, r])
        return carry

    lax.fori_loop(0, rows, step, 0)


def shifted_copies(volume, above, below):
    depths, rows, columns, pixels = volume.shape
    ext = rows + 2 * REACH
    return pl.pallas_call(
        shift_kernel,
        grid=(depths,),
        in_specs=[
            pl.BlockSpec((1, rows, columns, pixels), lambda d: (d, 0, 0, 0)),
            pl.BlockSpec((1, REACH, columns, pixels), lambda d: (d, 0, 0, 0)),
            pl.BlockSpec((1, REACH, columns, pixels), lambda d: (d, 0, 0, 0)),
        ],
        out_specs=pl.BlockSpec((SHIFTS, 1, ext, columns, pixels), lambda d: (0, d, 0, 0, 0)),
        out_shape=jax.ShapeDtypeStruct((SHIFTS, depths, ext, columns, pixels), jnp.bfloat16),
        compiler_params=pltpu.CompilerParams(vmem_limit_bytes=VMEM),
        name="shifted_copies",
    )(volume, above, below)


def project_kernel(place_ref, start_ref, w_ref, even_ref, odd_ref, meas_ref, dark_ref, pred_ref, ratio_ref):
    i = pl.program_id(0)
    rows, columns, pixels = pred_ref.shape
    dims = (((1,), (1,)), ((), ()))
    a = even_ref[0].reshape(rows * columns, pixels)
    b = odd_ref[0].reshape(rows * columns, pixels)
    w = w_ref[0]
    part = lax.dot_general(a, w[:, :pixels], dims, preferred_element_type=jnp.float32)
    part = part + lax.dot_general(b, w[:, pixels:], dims, preferred_element_type=jnp.float32)
    part = part.reshape(rows, columns, pixels)

    @pl.when(i == 0)
    def _():
        pred_ref[...] = part

    @pl.when(i > 0)
    def _():
        pred_ref[...] = pred_ref[...] + part

    @pl.when(i == pl.num_programs(0) - 1)
    def _():
        ratio_ref[...] = meas_ref[...] / (pred_ref[...] + dark_ref[...])


def project(copies, weights, place, start, measured, dark_level):
    rows, columns, pixels = measured.shape
    shards, _, pair = weights.shape
    whole = lambda i, *_: (0, 0, 0)

    def slab(which):
        return pl.BlockSpec(
            (pl.Element(1), pl.Element(rows), pl.Element(columns), pl.Element(pixels)),
            lambda i, place_ref, start_ref: (place_ref[2 * i + which], start_ref[2 * i + which], 0, 0),
        )

    grid_spec = pltpu.PrefetchScalarGridSpec(
        num_scalar_prefetch=2,
        grid=(shards,),
        in_specs=[
            pl.BlockSpec((1, pixels, pair), lambda i, *_: (i, 0, 0)),
            slab(0),
            slab(1),
            pl.BlockSpec((rows, columns, pixels), whole),
            pl.BlockSpec((1, 1, pixels), whole),
        ],
        out_specs=[pl.BlockSpec((rows, columns, pixels), whole)] * 2,
    )
    return pl.pallas_call(
        project_kernel,
        grid_spec=grid_spec,
        out_shape=[jax.ShapeDtypeStruct(measured.shape, jnp.float32)] * 2,
        compiler_params=pltpu.CompilerParams(vmem_limit_bytes=VMEM),
        name="project",
    )(place, start, weights, copies, copies, measured, dark_level.reshape(1, 1, pixels))


def gathered_pairs(operator_rows):
    held, pixels = operator_rows.shape
    if held == 2 * pixels:
        return lax.all_gather(operator_rows.T, "lenslet", axis=0)
    every = lax.all_gather(operator_rows, "lenslet", axis=0, tiled=True)
    return every.reshape(-1, 2 * pixels, pixels).transpose(0, 2, 1)


def body(volume, measured, operator_rows, offset_counts, offset_table, dark_level):
    depths, rows, columns, pixels = volume.shape
    op_total = offset_table.shape[0]
    planes = jnp.arange(depths, dtype=jnp.int32)
    ends = jnp.sum(jnp.where(planes[None, :] <= planes[:, None], offset_counts[None, :], 0), axis=1)
    positions = jnp.arange(op_total, dtype=jnp.int32)
    depth_of = jnp.sum((positions[:, None] >= ends[None, :]).astype(jnp.int32), axis=1)
    place = (offset_table[:, 1] + REACH) * depths + depth_of
    start = offset_table[:, 0] + REACH

    weights = gathered_pairs(operator_rows)
    above = passed_along(volume[:, rows - REACH :], "lenslet", 1)
    below = passed_along(volume[:, :REACH], "lenslet", -1)
    copies = shifted_copies(volume, above, below)
    copies = copies.reshape(SHIFTS * depths, rows + 2 * REACH, columns, pixels)
    return tuple(project(copies, weights, place, start, measured, dark_level))


def solution(mesh):
    placed = (
        P("frames", "lenslet", None, None),
        P(("frames", "lenslet"), None, None),
        P("lenslet", None),
        P(),
        P(),
        P(),
    )
    return jax.shard_map(
        body,
        mesh=mesh,
        in_specs=placed,
        out_specs=(P(("frames", "lenslet"), None, None), P(("frames", "lenslet"), None, None)),
        check_vma=False,
    )
```

```python
import functools

import jax
import jax.numpy as jnp
from jax import lax
from jax.experimental import pallas as pl
from jax.experimental.pallas import tpu as pltpu
from jax.sharding import PartitionSpec as P

REACH = 2
SHIFTS = 2 * REACH + 1
VMEM = 60 * 1024 * 1024
SMALL = 12 * 1024 * 1024
TILE = 8


def passed_along(block, axis, distance):
    devices = range(lax.axis_size(axis))
    route = [(i - distance, i) for i in devices if i - distance in devices]
    return lax.ppermute(block, axis, route)


def shift_kernel(own_ref, above_ref, below_ref, out_ref):
    rows, columns, pixels = own_ref.shape[1:]
    col = lax.broadcasted_iota(jnp.int32, (columns, pixels), 0)

    def put(row, plane):
        wide = plane.astype(jnp.float32)
        for s in range(SHIFTS):
            step = s - REACH
            if step == 0:
                moved = wide
            else:
                moved = pltpu.roll(wide, (-step) % columns, 0)
                inside = col < columns - step if step > 0 else col >= -step
                moved = jnp.where(inside, moved, 0.0)
            out_ref[s, 0, row] = moved.astype(jnp.bfloat16)

    for r in range(REACH):
        put(r, above_ref[0, r])
        put(rows + REACH + r, below_ref[0, r])

    def step(r, carry):
        put(r + REACH, own_ref[0, r])
        return carry

    lax.fori_loop(0, rows, step, 0)


def shifted_copies(volume, above, below):
    depths, rows, columns, pixels = volume.shape
    ext = rows + 2 * REACH
    return pl.pallas_call(
        shift_kernel,
        grid=(depths,),
        in_specs=[
            pl.BlockSpec((1, rows, columns, pixels), lambda d: (d, 0, 0, 0)),
            pl.BlockSpec((1, REACH, columns, pixels), lambda d: (d, 0, 0, 0)),
            pl.BlockSpec((1, REACH, columns, pixels), lambda d: (d, 0, 0, 0)),
        ],
        out_specs=pl.BlockSpec((SHIFTS, 1, ext, columns, pixels), lambda d: (0, d, 0, 0, 0)),
        out_shape=jax.ShapeDtypeStruct((SHIFTS, depths, ext, columns, pixels), jnp.bfloat16),
        compiler_params=pltpu.CompilerParams(vmem_limit_bytes=VMEM),
        name="shifted_copies",
    )(volume, above, below)


def project_kernel(place_ref, start_ref, w_ref, even_ref, odd_ref, meas_ref, dark_ref, pred_ref, ratio_ref):
    i = pl.program_id(0)
    rows, columns, pixels = pred_ref.shape
    dims = (((1,), (1,)), ((), ()))
    a = even_ref[0].reshape(rows * columns, pixels)
    b = odd_ref[0].reshape(rows * columns, pixels)
    w = w_ref[0]
    part = lax.dot_general(a, w[:, :pixels], dims, preferred_element_type=jnp.float32)
    part = part + lax.dot_general(b, w[:, pixels:], dims, preferred_element_type=jnp.float32)
    part = part.reshape(rows, columns, pixels)

    @pl.when(i == 0)
    def _():
        pred_ref[...] = part

    @pl.when(i > 0)
    def _():
        pred_ref[...] = pred_ref[...] + part

    @pl.when(i == pl.num_programs(0) - 1)
    def _():
        ratio_ref[...] = meas_ref[...] / (pred_ref[...] + dark_ref[...])


def project(copies, weights, place, start, measured, dark_level):
    rows, columns, pixels = measured.shape
    shards, _, pair = weights.shape
    whole = lambda i, *_: (0, 0, 0)

    def slab(which):
        return pl.BlockSpec(
            (pl.Element(1), pl.Element(rows), pl.Element(columns), pl.Element(pixels)),
            lambda i, place_ref, start_ref: (
                place_ref[jnp.minimum(2 * i + which, 2 * shards - 1)],
                start_ref[jnp.minimum(2 * i + which, 2 * shards - 1)],
                0,
                0,
            ),
        )

    grid_spec = pltpu.PrefetchScalarGridSpec(
        num_scalar_prefetch=2,
        grid=(shards,),
        in_specs=[
            pl.BlockSpec((1, pixels, pair), lambda i, *_: (i, 0, 0)),
            slab(0),
            slab(1),
            pl.BlockSpec((rows, columns, pixels), whole),
            pl.BlockSpec((1, 1, pixels), whole),
        ],
        out_specs=[pl.BlockSpec((rows, columns, pixels), whole)] * 2,
    )
    return pl.pallas_call(
        project_kernel,
        grid_spec=grid_spec,
        out_shape=[jax.ShapeDtypeStruct(measured.shape, jnp.float32)] * 2,
        compiler_params=pltpu.CompilerParams(vmem_limit_bytes=VMEM),
        name="project",
    )(place, start, weights, copies, copies, measured, dark_level.reshape(1, 1, pixels))


def gathered_pairs(operator_rows):
    held, pixels = operator_rows.shape
    if held == 2 * pixels:
        return lax.all_gather(operator_rows.T, "lenslet", axis=0)
    every = lax.all_gather(operator_rows, "lenslet", axis=0, tiled=True)
    return every.reshape(-1, 2 * pixels, pixels).transpose(0, 2, 1)


IN_VMEM = pl.BlockSpec(memory_space=pltpu.VMEM)
IN_SMEM = pl.BlockSpec(memory_space=pltpu.SMEM)
IN_HBM = pl.BlockSpec(memory_space=pl.ANY)


def put_shifted(out_ref, depth, row, plane):
    columns, pixels = plane.shape
    wide = plane.astype(jnp.float32)
    col = lax.broadcasted_iota(jnp.int32, (columns, pixels), 0)
    depths = out_ref.shape[0] // SHIFTS
    for s in range(SHIFTS):
        step = s - REACH
        if step == 0:
            out_ref[s * depths + depth, row] = plane
            continue
        moved = pltpu.roll(wide, (-step) % columns, 0)
        inside = col < columns - step if step > 0 else col >= -step
        out_ref[s * depths + depth, row] = jnp.where(inside, moved, 0.0).astype(jnp.bfloat16)


def own_rows_kernel(volume_ref, out_ref):
    depths, rows, _, _ = volume_ref.shape

    def step(n, carry):
        d, r = n // rows, n % rows
        put_shifted(out_ref, d, r + REACH, volume_ref[d, r])
        return carry

    lax.fori_loop(0, depths * rows, step, 0)


def edge_rows_kernel(above_ref, below_ref, old_ref, out_ref):
    depths, reach, _, _ = above_ref.shape
    rows = out_ref.shape[1] - 2 * reach

    def step(n, carry):
        d, r = n // reach, n % reach
        put_shifted(out_ref, d, r, above_ref[d, r])
        put_shifted(out_ref, d, r + rows + reach, below_ref[d, r])
        return carry

    lax.fori_loop(0, depths * reach, step, 0)


def own_rows(volume):
    depths, rows, columns, pixels = volume.shape
    return pl.pallas_call(
        own_rows_kernel,
        in_specs=[IN_VMEM],
        out_specs=IN_VMEM,
        out_shape=pltpu.VMEM((SHIFTS * depths, rows + 2 * REACH, columns, pixels), jnp.bfloat16),
        compiler_params=pltpu.CompilerParams(vmem_limit_bytes=SMALL),
        cost_estimate=pl.CostEstimate(flops=0, bytes_accessed=10 * 1024 * 1024, transcendentals=0),
        name="own_rows",
    )(volume)


def edge_rows(above, below, copies):
    return pl.pallas_call(
        edge_rows_kernel,
        in_specs=[IN_VMEM, IN_VMEM, IN_VMEM],
        out_specs=IN_VMEM,
        out_shape=pltpu.VMEM(copies.shape, copies.dtype),
        input_output_aliases={2: 0},
        compiler_params=pltpu.CompilerParams(vmem_limit_bytes=SMALL),
        name="edge_rows",
    )(above, below, copies)


def operator_spot(scalars, op, depths):
    end, depth = jnp.int32(0), jnp.int32(0)
    for d in range(depths):
        end = end + scalars[d]
        depth = depth + jnp.where(op >= end, 1, 0)
    at = depths + 2 * op
    return (scalars[at + 1] + REACH) * depths + depth, scalars[at] + REACH


def add_kernel(scalars, copies, *refs, plan, pieces, first, last):
    weights = refs[: 2 * pieces]
    refs = refs[2 * pieces :]
    if last:
        meas, dark, old, pred_out, ratio_out, acc, pred, ratio, sems = refs
    elif first:
        old, acc = None, refs[0]
    else:
        old, acc = refs
    depths = copies.shape[0] // SHIFTS
    columns, pixels = copies.shape[2:]
    lines = acc.shape[1]
    rows = lines // columns
    here, side = scalars[scalars.shape[0] - 2], scalars[scalars.shape[0] - 1]
    dims = (((1,), (1,)), ((), ()))
    jobs = []
    for n, (hops, other, kind) in enumerate(plan):
        shard = ((here + (16 - 4 * hops)) % 16) ^ (2 * other)
        half = n if kind is None else side ^ kind
        spots = []
        for core in range(2):
            for which in range(2):
                spots.append(operator_spot(scalars, 2 * (shard ^ core) + which, depths))
        jobs.append((n, half, spots))

    for t in range(rows // TILE):
        m = slice(t * TILE * columns, (t + 1) * TILE * columns)
        for n, half, spots in jobs:
            total = None
            for j, (copy, row) in enumerate(spots):
                w_ref = weights[2 * n + j // 2]
                w = w_ref[0] if w_ref.shape[0] == 1 else w_ref[n]
                w = w[:, pixels * (j % 2) : pixels * (j % 2 + 1)]
                slab = copies[copy, pl.ds(row + t * TILE, TILE)].reshape(TILE * columns, pixels)
                part = lax.dot_general(slab, w, dims, preferred_element_type=jnp.float32)
                total = part if total is None else total + part
            if first:
                acc[half, m] = total
            elif last and n == 0:
                acc[half, m] = old[half, m] + total
                acc[1 - half, m] = old[1 - half, m]
            elif last:
                acc[half, m] = acc[half, m] + total
            else:
                acc[half, m] = acc[half, m] + total if n else old[half, m] + total
        if last:
            r = slice(t * TILE, (t + 1) * TILE)
            full = jnp.concatenate([acc[0, m], acc[1, m]], axis=1).reshape(TILE, columns, pixels)
            pred[r] = full
            ratio[r] = meas[r] / (full + dark[...].reshape(1, 1, pixels))
            for q, (src, dst) in enumerate(((pred, pred_out), (ratio, ratio_out))):
                pltpu.make_async_copy(src.at[r], dst.at[r], sems.at[2 * t + q]).start()
    if last:
        for t in range(rows // TILE):
            r = slice(t * TILE, (t + 1) * TILE)
            for q, (src, dst) in enumerate(((pred, pred_out), (ratio, ratio_out))):
                pltpu.make_async_copy(src.at[r], dst.at[r], sems.at[2 * t + q]).wait()


def add_pieces(scalars, copies, weights, plan, acc, final=None):
    columns, pixels = copies.shape[2:]
    rows = copies.shape[1] - 2 * REACH
    lines, part = rows * columns, pixels // 2
    pieces = len(plan)
    operands = [scalars, copies, *weights]
    shape = (2, lines, part)
    scratch, params = [], {}
    alias = {}
    if final is not None:
        operands += [*final, acc]
        full = final[0].shape
        out_shape = [jax.ShapeDtypeStruct(full, jnp.float32)] * 2
        out_specs = [IN_HBM] * 2
        scratch = [pltpu.VMEM(shape, jnp.float32), pltpu.VMEM(full, jnp.float32), pltpu.VMEM(full, jnp.float32)]
        scratch.append(pltpu.SemaphoreType.DMA((2 * (rows // TILE),)))
    else:
        out_shape, out_specs = pltpu.VMEM(shape, jnp.float32), IN_VMEM
        if acc is not None:
            alias = {len(operands): 0}
            operands.append(acc)
    flops = 2 * lines * 4 * pixels * part * pieces
    return pl.pallas_call(
        functools.partial(add_kernel, plan=plan, pieces=pieces, first=acc is None, last=final is not None),
        in_specs=[IN_SMEM] + [IN_VMEM] * (len(operands) - 1),
        out_specs=out_specs,
        out_shape=out_shape,
        scratch_shapes=scratch,
        input_output_aliases=alias,
        cost_estimate=pl.CostEstimate(flops=flops, bytes_accessed=pieces * 1024 * 1024, transcendentals=0),
        compiler_params=pltpu.CompilerParams(vmem_limit_bytes=SMALL),
        name="add_pieces",
    )(*operands)


def placements(offset_counts, offset_table):
    depths = offset_counts.shape[0]
    planes = jnp.arange(depths, dtype=jnp.int32)
    ends = jnp.sum(jnp.where(planes[None, :] <= planes[:, None], offset_counts[None, :], 0), axis=1)
    positions = jnp.arange(offset_table.shape[0], dtype=jnp.int32)
    depth_of = jnp.sum((positions[:, None] >= ends[None, :]).astype(jnp.int32), axis=1)
    return (offset_table[:, 1] + REACH) * depths + depth_of, offset_table[:, 0] + REACH


def exchanged(volume, measured, operator_rows, offset_counts, offset_table, dark_level):
    depths, rows, columns, pixels = volume.shape
    part = pixels // 2
    side = lax.axis_index("frames")
    here = lax.axis_index("lenslet")
    count = lax.axis_size("lenslet")
    scalars = jnp.concatenate([offset_counts, offset_table.reshape(-1), jnp.stack([here, side])])

    up = [(i, (i + 4) % count) for i in range(count)]
    beside = [(i, i ^ 2) for i in range(count)]
    twin = [(i, i ^ 1) for i in range(count)]
    along_z = lambda v: lax.ppermute(v, "lenslet", up)
    along_y = lambda v: lax.ppermute(v, "lenslet", beside)
    to_core = lambda v: lax.ppermute(v, "lenslet", twin)
    along_x = lambda v: lax.ppermute(v, "frames", [(0, 1), (1, 0)])

    own = operator_rows.T.reshape(2, part, 2 * pixels)
    own_a = lax.dynamic_index_in_dim(own, side, 0)
    own_b = lax.dynamic_index_in_dim(own, 1 - side, 0)
    both = lambda *pieces: [w for piece in pieces for w in (piece, to_core(piece))]

    t1a, y0a = along_z(own_a), along_y(own_a)
    above = passed_along(volume[:, rows - REACH :], "lenslet", 1)
    below = passed_along(volume[:, :REACH], "lenslet", -1)
    own_c = to_core(own)
    copies = own_rows(volume)
    t2a, y1a, y0b = along_z(t1a), along_y(t1a), along_x(y0a)
    r0 = both(t1a, y0a)
    copies = edge_rows(above, below, copies)
    a, b = 0, 1
    acc = add_pieces(scalars, copies, [own, own_c, own, own_c], [(0, 0, None), (0, 0, None)], None)
    t3a, y2a, y1b = along_z(t2a), along_y(t2a), along_x(y1a)
    r1 = both(t2a, y1a, y0b)
    acc = add_pieces(scalars, copies, r0, [(1, 0, a), (0, 1, a)], acc)
    t1b, y3a, t2b = along_z(own_b), along_y(t3a), along_x(t2a)
    r2 = both(t3a, y2a, y1b)
    acc = add_pieces(scalars, copies, r1, [(2, 0, a), (1, 1, a), (0, 1, b)], acc)
    t3b, y2b, y3b = along_z(t2b), along_y(t2b), along_x(y3a)
    r3 = both(t1b, y3a, t2b)
    acc = add_pieces(scalars, copies, r2, [(3, 0, a), (2, 1, a), (1, 1, b)], acc)
    r4 = both(t3b, y2b, y3b)
    acc = add_pieces(scalars, copies, r3, [(1, 0, b), (3, 1, a), (2, 0, b)], acc)
    final = (measured, dark_level.reshape(1, pixels))
    return tuple(add_pieces(scalars, copies, r4, [(3, 0, b), (2, 1, b), (3, 1, b)], acc, final))


def gathered(volume, measured, operator_rows, offset_counts, offset_table, dark_level):
    depths, rows, columns, pixels = volume.shape
    place, start = placements(offset_counts, offset_table)
    weights = gathered_pairs(operator_rows)
    above = passed_along(volume[:, rows - REACH :], "lenslet", 1)
    below = passed_along(volume[:, :REACH], "lenslet", -1)
    copies = shifted_copies(volume, above, below)
    copies = copies.reshape(SHIFTS * depths, rows + 2 * REACH, columns, pixels)
    return tuple(project(copies, weights, place, start, measured, dark_level))


def body(volume, measured, operator_rows, offset_counts, offset_table, dark_level):
    pairs = operator_rows.shape[0] == 2 * operator_rows.shape[1]
    known = lax.axis_size("lenslet") == 16 and lax.axis_size("frames") == 2
    form = exchanged if pairs and known else gathered
    return form(volume, measured, operator_rows, offset_counts, offset_table, dark_level)


def solution(mesh):
    placed = (
        P("frames", "lenslet", None, None),
        P(("frames", "lenslet"), None, None),
        P("lenslet", None),
        P(),
        P(),
        P(),
    )
    return jax.shard_map(
        body,
        mesh=mesh,
        in_specs=placed,
        out_specs=(P(("frames", "lenslet"), None, None), P(("frames", "lenslet"), None, None)),
        check_vma=False,
    )
```

```python
import functools

import jax
import jax.numpy as jnp
from jax import lax
from jax.experimental import pallas as pl
from jax.experimental.pallas import tpu as pltpu
from jax.sharding import PartitionSpec as P

REACH = 2
SHIFTS = 2 * REACH + 1
VMEM = 60 * 1024 * 1024
SMALL = 12 * 1024 * 1024
TILE = 8


def passed_along(block, axis, distance):
    devices = range(lax.axis_size(axis))
    route = [(i - distance, i) for i in devices if i - distance in devices]
    return lax.ppermute(block, axis, route)


def shift_kernel(own_ref, above_ref, below_ref, out_ref):
    rows, columns, pixels = own_ref.shape[1:]
    col = lax.broadcasted_iota(jnp.int32, (columns, pixels), 0)

    def put(row, plane):
        wide = plane.astype(jnp.float32)
        for s in range(SHIFTS):
            step = s - REACH
            if step == 0:
                moved = wide
            else:
                moved = pltpu.roll(wide, (-step) % columns, 0)
                inside = col < columns - step if step > 0 else col >= -step
                moved = jnp.where(inside, moved, 0.0)
            out_ref[s, 0, row] = moved.astype(jnp.bfloat16)

    for r in range(REACH):
        put(r, above_ref[0, r])
        put(rows + REACH + r, below_ref[0, r])

    def step(r, carry):
        put(r + REACH, own_ref[0, r])
        return carry

    lax.fori_loop(0, rows, step, 0)


def shifted_copies(volume, above, below):
    depths, rows, columns, pixels = volume.shape
    ext = rows + 2 * REACH
    return pl.pallas_call(
        shift_kernel,
        grid=(depths,),
        in_specs=[
            pl.BlockSpec((1, rows, columns, pixels), lambda d: (d, 0, 0, 0)),
            pl.BlockSpec((1, REACH, columns, pixels), lambda d: (d, 0, 0, 0)),
            pl.BlockSpec((1, REACH, columns, pixels), lambda d: (d, 0, 0, 0)),
        ],
        out_specs=pl.BlockSpec((SHIFTS, 1, ext, columns, pixels), lambda d: (0, d, 0, 0, 0)),
        out_shape=jax.ShapeDtypeStruct((SHIFTS, depths, ext, columns, pixels), jnp.bfloat16),
        compiler_params=pltpu.CompilerParams(vmem_limit_bytes=VMEM),
        name="shifted_copies",
    )(volume, above, below)


def project_kernel(place_ref, start_ref, w_ref, even_ref, odd_ref, meas_ref, dark_ref, pred_ref, ratio_ref):
    i = pl.program_id(0)
    rows, columns, pixels = pred_ref.shape
    dims = (((1,), (1,)), ((), ()))
    a = even_ref[0].reshape(rows * columns, pixels)
    b = odd_ref[0].reshape(rows * columns, pixels)
    w = w_ref[0]
    part = lax.dot_general(a, w[:, :pixels], dims, preferred_element_type=jnp.float32)
    part = part + lax.dot_general(b, w[:, pixels:], dims, preferred_element_type=jnp.float32)
    part = part.reshape(rows, columns, pixels)

    @pl.when(i == 0)
    def _():
        pred_ref[...] = part

    @pl.when(i > 0)
    def _():
        pred_ref[...] = pred_ref[...] + part

    @pl.when(i == pl.num_programs(0) - 1)
    def _():
        ratio_ref[...] = meas_ref[...] / (pred_ref[...] + dark_ref[...])


def project(copies, weights, place, start, measured, dark_level):
    rows, columns, pixels = measured.shape
    shards, _, pair = weights.shape
    whole = lambda i, *_: (0, 0, 0)

    def slab(which):
        return pl.BlockSpec(
            (pl.Element(1), pl.Element(rows), pl.Element(columns), pl.Element(pixels)),
            lambda i, place_ref, start_ref: (
                place_ref[jnp.minimum(2 * i + which, 2 * shards - 1)],
                start_ref[jnp.minimum(2 * i + which, 2 * shards - 1)],
                0,
                0,
            ),
        )

    grid_spec = pltpu.PrefetchScalarGridSpec(
        num_scalar_prefetch=2,
        grid=(shards,),
        in_specs=[
            pl.BlockSpec((1, pixels, pair), lambda i, *_: (i, 0, 0)),
            slab(0),
            slab(1),
            pl.BlockSpec((rows, columns, pixels), whole),
            pl.BlockSpec((1, 1, pixels), whole),
        ],
        out_specs=[pl.BlockSpec((rows, columns, pixels), whole)] * 2,
    )
    return pl.pallas_call(
        project_kernel,
        grid_spec=grid_spec,
        out_shape=[jax.ShapeDtypeStruct(measured.shape, jnp.float32)] * 2,
        compiler_params=pltpu.CompilerParams(vmem_limit_bytes=VMEM),
        name="project",
    )(place, start, weights, copies, copies, measured, dark_level.reshape(1, 1, pixels))


def gathered_pairs(operator_rows):
    held, pixels = operator_rows.shape
    if held == 2 * pixels:
        return lax.all_gather(operator_rows.T, "lenslet", axis=0)
    every = lax.all_gather(operator_rows, "lenslet", axis=0, tiled=True)
    return every.reshape(-1, 2 * pixels, pixels).transpose(0, 2, 1)


IN_VMEM = pl.BlockSpec(memory_space=pltpu.VMEM)
IN_SMEM = pl.BlockSpec(memory_space=pltpu.SMEM)
IN_HBM = pl.BlockSpec(memory_space=pl.ANY)


def put_shifted(out_ref, depth, row, plane):
    columns, pixels = plane.shape
    wide = plane.astype(jnp.float32)
    col = lax.broadcasted_iota(jnp.int32, (columns, pixels), 0)
    depths = out_ref.shape[0] // SHIFTS
    for s in range(SHIFTS):
        step = s - REACH
        if step == 0:
            out_ref[s * depths + depth, row] = plane
            continue
        moved = pltpu.roll(wide, (-step) % columns, 0)
        inside = col < columns - step if step > 0 else col >= -step
        out_ref[s * depths + depth, row] = jnp.where(inside, moved, 0.0).astype(jnp.bfloat16)


def own_rows_kernel(volume_ref, out_ref, held, sems):
    depths, rows, _, _ = held.shape
    fetch = [pltpu.make_async_copy(volume_ref.at[d], held.at[d], sems.at[d]) for d in range(depths)]
    for copy in fetch:
        copy.start()
    for d, copy in enumerate(fetch):
        copy.wait()

        def step(r, carry, d=d):
            put_shifted(out_ref, d, r + REACH, held[d, r])
            return carry

        lax.fori_loop(0, rows, step, 0)


def edge_rows_kernel(above_ref, below_ref, old_ref, out_ref):
    depths, reach, _, _ = above_ref.shape
    rows = out_ref.shape[1] - 2 * reach

    def step(n, carry):
        d, r = n // reach, n % reach
        put_shifted(out_ref, d, r, above_ref[d, r])
        put_shifted(out_ref, d, r + rows + reach, below_ref[d, r])
        return carry

    lax.fori_loop(0, depths * reach, step, 0)


def own_rows(volume):
    depths, rows, columns, pixels = volume.shape
    shape = (SHIFTS * depths, rows + 2 * REACH, columns, pixels)
    return pl.pallas_call(
        own_rows_kernel,
        in_specs=[pl.BlockSpec(memory_space=pltpu.HBM)],
        scratch_shapes=[pltpu.VMEM(volume.shape, volume.dtype), pltpu.SemaphoreType.DMA((depths,))],
        out_specs=IN_VMEM,
        out_shape=pltpu.VMEM(shape, volume.dtype),
        compiler_params=pltpu.CompilerParams(vmem_limit_bytes=SMALL),
        name="own_rows",
    )(pltpu.with_memory_space_constraint(volume, pltpu.HBM))


def edge_rows(above, below, copies):
    return pl.pallas_call(
        edge_rows_kernel,
        in_specs=[IN_VMEM, IN_VMEM, IN_VMEM],
        out_specs=IN_VMEM,
        out_shape=pltpu.VMEM(copies.shape, copies.dtype),
        input_output_aliases={2: 0},
        compiler_params=pltpu.CompilerParams(vmem_limit_bytes=SMALL),
        name="edge_rows",
    )(above, below, copies)


def operator_spot(scalars, op, depths):
    end, depth = jnp.int32(0), jnp.int32(0)
    for d in range(depths):
        end = end + scalars[d]
        depth = depth + jnp.where(op >= end, 1, 0)
    at = depths + 2 * op
    return (scalars[at + 1] + REACH) * depths + depth, scalars[at] + REACH


def add_kernel(scalars, copies, *refs, plan, pieces, first, last):
    weights = refs[: 2 * pieces]
    refs = refs[2 * pieces :]
    if last:
        meas, dark, old, pred_out, ratio_out, acc, pred, ratio, sems = refs
    elif first:
        old, acc = None, refs[0]
    else:
        old, acc = refs
    depths = copies.shape[0] // SHIFTS
    columns, pixels = copies.shape[2:]
    lines = acc.shape[1]
    rows = lines // columns
    here, side = scalars[scalars.shape[0] - 2], scalars[scalars.shape[0] - 1]
    dims = (((1,), (1,)), ((), ()))
    jobs = []
    for n, (hops, other, kind) in enumerate(plan):
        shard = ((here + (16 - 4 * hops)) % 16) ^ (2 * other)
        half = n if kind is None else side ^ kind
        spots = []
        for core in range(2):
            for which in range(2):
                spots.append(operator_spot(scalars, 2 * (shard ^ core) + which, depths))
        jobs.append((n, half, spots))

    for t in range(rows // TILE):
        m = slice(t * TILE * columns, (t + 1) * TILE * columns)
        for n, half, spots in jobs:
            total = None
            for j, (copy, row) in enumerate(spots):
                w_ref = weights[2 * n + j // 2]
                w = w_ref[0] if w_ref.shape[0] == 1 else w_ref[n]
                w = w[:, pixels * (j % 2) : pixels * (j % 2 + 1)]
                slab = copies[copy, pl.ds(row + t * TILE, TILE)].reshape(TILE * columns, pixels)
                part = lax.dot_general(slab, w, dims, preferred_element_type=jnp.float32)
                total = part if total is None else total + part
            if first:
                acc[half, m] = total
            elif last and n == 0:
                acc[half, m] = old[half, m] + total
                acc[1 - half, m] = old[1 - half, m]
            elif last:
                acc[half, m] = acc[half, m] + total
            else:
                acc[half, m] = acc[half, m] + total if n else old[half, m] + total
        if last:
            r = slice(t * TILE, (t + 1) * TILE)
            full = jnp.concatenate([acc[0, m], acc[1, m]], axis=1).reshape(TILE, columns, pixels)
            pred[r] = full
            ratio[r] = meas[r] / (full + dark[...].reshape(1, 1, pixels))
            for q, (src, dst) in enumerate(((pred, pred_out), (ratio, ratio_out))):
                pltpu.make_async_copy(src.at[r], dst.at[r], sems.at[2 * t + q]).start()
    if last:
        for t in range(rows // TILE):
            r = slice(t * TILE, (t + 1) * TILE)
            for q, (src, dst) in enumerate(((pred, pred_out), (ratio, ratio_out))):
                pltpu.make_async_copy(src.at[r], dst.at[r], sems.at[2 * t + q]).wait()


def add_pieces(scalars, copies, weights, plan, acc, final=None):
    columns, pixels = copies.shape[2:]
    rows = copies.shape[1] - 2 * REACH
    lines, part = rows * columns, pixels // 2
    pieces = len(plan)
    operands = [scalars, copies, *weights]
    shape = (2, lines, part)
    scratch, params = [], {}
    alias = {}
    if final is not None:
        operands += [*final, acc]
        full = final[0].shape
        out_shape = [jax.ShapeDtypeStruct(full, jnp.float32)] * 2
        out_specs = [IN_HBM] * 2
        scratch = [pltpu.VMEM(shape, jnp.float32), pltpu.VMEM(full, jnp.float32), pltpu.VMEM(full, jnp.float32)]
        scratch.append(pltpu.SemaphoreType.DMA((2 * (rows // TILE),)))
    else:
        out_shape, out_specs = pltpu.VMEM(shape, jnp.float32), IN_VMEM
        if acc is not None:
            alias = {len(operands): 0}
            operands.append(acc)
    flops = 2 * lines * 4 * pixels * part * pieces
    return pl.pallas_call(
        functools.partial(add_kernel, plan=plan, pieces=pieces, first=acc is None, last=final is not None),
        in_specs=[IN_SMEM] + [IN_VMEM] * (len(operands) - 1),
        out_specs=out_specs,
        out_shape=out_shape,
        scratch_shapes=scratch,
        input_output_aliases=alias,
        cost_estimate=pl.CostEstimate(flops=flops, bytes_accessed=pieces * 1024 * 1024, transcendentals=0),
        compiler_params=pltpu.CompilerParams(vmem_limit_bytes=SMALL),
        name="add_pieces",
    )(*operands)


def placements(offset_counts, offset_table):
    depths = offset_counts.shape[0]
    planes = jnp.arange(depths, dtype=jnp.int32)
    ends = jnp.sum(jnp.where(planes[None, :] <= planes[:, None], offset_counts[None, :], 0), axis=1)
    positions = jnp.arange(offset_table.shape[0], dtype=jnp.int32)
    depth_of = jnp.sum((positions[:, None] >= ends[None, :]).astype(jnp.int32), axis=1)
    return (offset_table[:, 1] + REACH) * depths + depth_of, offset_table[:, 0] + REACH


def exchanged(volume, measured, operator_rows, offset_counts, offset_table, dark_level):
    depths, rows, columns, pixels = volume.shape
    part = pixels // 2
    side = lax.axis_index("frames")
    here = lax.axis_index("lenslet")
    count = lax.axis_size("lenslet")
    scalars = jnp.concatenate([offset_counts, offset_table.reshape(-1), jnp.stack([here, side])])

    up = [(i, (i + 4) % count) for i in range(count)]
    beside = [(i, i ^ 2) for i in range(count)]
    twin = [(i, i ^ 1) for i in range(count)]
    along_z = lambda v: lax.ppermute(v, "lenslet", up)
    along_y = lambda v: lax.ppermute(v, "lenslet", beside)
    to_core = lambda v: lax.ppermute(v, "lenslet", twin)
    along_x = lambda v: lax.ppermute(v, "frames", [(0, 1), (1, 0)])

    own = operator_rows.T.reshape(2, part, 2 * pixels)
    own_a = lax.dynamic_index_in_dim(own, side, 0)
    own_b = lax.dynamic_index_in_dim(own, 1 - side, 0)
    both = lambda *pieces: [w for piece in pieces for w in (piece, to_core(piece))]

    tied = lax.optimization_barrier
    a, b = 0, 1
    t1a, y0a = along_z(own_a), along_y(own_a)
    above = passed_along(volume[:, rows - REACH :], "lenslet", 1)
    below = passed_along(volume[:, :REACH], "lenslet", -1)
    own_c = to_core(own)
    volume, scalars, own_b = tied((volume, scalars, own_b))
    copies = own_rows(volume)
    t1a, y0a, above, below, own_c, copies = tied((t1a, y0a, above, below, own_c, copies))
    t2a, y1a, y0b = along_z(t1a), along_y(t1a), along_x(y0a)
    r0 = both(t1a, y0a)
    copies = edge_rows(above, below, copies)
    acc = add_pieces(scalars, copies, [own, own_c, own, own_c], [(0, 0, None), (0, 0, None)], None)
    acc = add_pieces(scalars, copies, r0, [(1, 0, a), (0, 1, a)], acc)
    t2a, y1a, y0b, acc = tied((t2a, y1a, y0b, acc))
    t3a, y2a, y1b = along_z(t2a), along_y(t2a), along_x(y1a)
    r1 = both(t2a, y1a, y0b)
    acc = add_pieces(scalars, copies, r1, [(2, 0, a), (1, 1, a), (0, 1, b)], acc)
    t3a, y2a, y1b, acc = tied((t3a, y2a, y1b, acc))
    t1b, y3a, t2b = along_z(own_b), along_y(t3a), along_x(t2a)
    r2 = both(t3a, y2a, y1b)
    acc = add_pieces(scalars, copies, r2, [(3, 0, a), (2, 1, a), (1, 1, b)], acc)
    t1b, y3a, t2b, acc = tied((t1b, y3a, t2b, acc))
    t3b, y2b, y3b = along_z(t2b), along_y(t2b), along_x(y3a)
    r3 = both(t1b, y3a, t2b)
    acc = add_pieces(scalars, copies, r3, [(1, 0, b), (3, 1, a), (2, 0, b)], acc)
    t3b, y2b, y3b, acc = tied((t3b, y2b, y3b, acc))
    r4 = both(t3b, y2b, y3b)
    final = (measured, dark_level.reshape(1, pixels))
    return tuple(add_pieces(scalars, copies, r4, [(3, 0, b), (2, 1, b), (3, 1, b)], acc, final))


def gathered(volume, measured, operator_rows, offset_counts, offset_table, dark_level):
    depths, rows, columns, pixels = volume.shape
    place, start = placements(offset_counts, offset_table)
    weights = gathered_pairs(operator_rows)
    above = passed_along(volume[:, rows - REACH :], "lenslet", 1)
    below = passed_along(volume[:, :REACH], "lenslet", -1)
    copies = shifted_copies(volume, above, below)
    copies = copies.reshape(SHIFTS * depths, rows + 2 * REACH, columns, pixels)
    return tuple(project(copies, weights, place, start, measured, dark_level))


def body(volume, measured, operator_rows, offset_counts, offset_table, dark_level):
    pairs = operator_rows.shape[0] == 2 * operator_rows.shape[1]
    known = lax.axis_size("lenslet") == 16 and lax.axis_size("frames") == 2
    form = exchanged if pairs and known else gathered
    return form(volume, measured, operator_rows, offset_counts, offset_table, dark_level)


def solution(mesh):
    placed = (
        P("frames", "lenslet", None, None),
        P(("frames", "lenslet"), None, None),
        P("lenslet", None),
        P(),
        P(),
        P(),
    )
    return jax.shard_map(
        body,
        mesh=mesh,
        in_specs=placed,
        out_specs=(P(("frames", "lenslet"), None, None), P(("frames", "lenslet"), None, None)),
        check_vma=False,
    )
```

```python
import functools

import jax
import jax.numpy as jnp
from jax import lax
from jax.experimental import pallas as pl
from jax.experimental.pallas import tpu as pltpu
from jax.sharding import PartitionSpec as P

REACH = 2
SHIFTS = 2 * REACH + 1
VMEM = 60 * 1024 * 1024
SMALL = 12 * 1024 * 1024
TILE = 8


def passed_along(block, axis, distance):
    devices = range(lax.axis_size(axis))
    route = [(i - distance, i) for i in devices if i - distance in devices]
    return lax.ppermute(block, axis, route)


def shift_kernel(own_ref, above_ref, below_ref, out_ref):
    rows, columns, pixels = own_ref.shape[1:]
    col = lax.broadcasted_iota(jnp.int32, (columns, pixels), 0)

    def put(row, plane):
        wide = plane.astype(jnp.float32)
        for s in range(SHIFTS):
            step = s - REACH
            if step == 0:
                moved = wide
            else:
                moved = pltpu.roll(wide, (-step) % columns, 0)
                inside = col < columns - step if step > 0 else col >= -step
                moved = jnp.where(inside, moved, 0.0)
            out_ref[s, 0, row] = moved.astype(jnp.bfloat16)

    for r in range(REACH):
        put(r, above_ref[0, r])
        put(rows + REACH + r, below_ref[0, r])

    def step(r, carry):
        put(r + REACH, own_ref[0, r])
        return carry

    lax.fori_loop(0, rows, step, 0)


def shifted_copies(volume, above, below):
    depths, rows, columns, pixels = volume.shape
    ext = rows + 2 * REACH
    return pl.pallas_call(
        shift_kernel,
        grid=(depths,),
        in_specs=[
            pl.BlockSpec((1, rows, columns, pixels), lambda d: (d, 0, 0, 0)),
            pl.BlockSpec((1, REACH, columns, pixels), lambda d: (d, 0, 0, 0)),
            pl.BlockSpec((1, REACH, columns, pixels), lambda d: (d, 0, 0, 0)),
        ],
        out_specs=pl.BlockSpec((SHIFTS, 1, ext, columns, pixels), lambda d: (0, d, 0, 0, 0)),
        out_shape=jax.ShapeDtypeStruct((SHIFTS, depths, ext, columns, pixels), jnp.bfloat16),
        compiler_params=pltpu.CompilerParams(vmem_limit_bytes=VMEM),
        name="shifted_copies",
    )(volume, above, below)


def project_kernel(place_ref, start_ref, w_ref, even_ref, odd_ref, meas_ref, dark_ref, pred_ref, ratio_ref):
    i = pl.program_id(0)
    rows, columns, pixels = pred_ref.shape
    dims = (((1,), (1,)), ((), ()))
    a = even_ref[0].reshape(rows * columns, pixels)
    b = odd_ref[0].reshape(rows * columns, pixels)
    w = w_ref[0]
    part = lax.dot_general(a, w[:, :pixels], dims, preferred_element_type=jnp.float32)
    part = part + lax.dot_general(b, w[:, pixels:], dims, preferred_element_type=jnp.float32)
    part = part.reshape(rows, columns, pixels)

    @pl.when(i == 0)
    def _():
        pred_ref[...] = part

    @pl.when(i > 0)
    def _():
        pred_ref[...] = pred_ref[...] + part

    @pl.when(i == pl.num_programs(0) - 1)
    def _():
        ratio_ref[...] = meas_ref[...] / (pred_ref[...] + dark_ref[...])


def project(copies, weights, place, start, measured, dark_level):
    rows, columns, pixels = measured.shape
    shards, _, pair = weights.shape
    whole = lambda i, *_: (0, 0, 0)

    def slab(which):
        return pl.BlockSpec(
            (pl.Element(1), pl.Element(rows), pl.Element(columns), pl.Element(pixels)),
            lambda i, place_ref, start_ref: (
                place_ref[jnp.minimum(2 * i + which, 2 * shards - 1)],
                start_ref[jnp.minimum(2 * i + which, 2 * shards - 1)],
                0,
                0,
            ),
        )

    grid_spec = pltpu.PrefetchScalarGridSpec(
        num_scalar_prefetch=2,
        grid=(shards,),
        in_specs=[
            pl.BlockSpec((1, pixels, pair), lambda i, *_: (i, 0, 0)),
            slab(0),
            slab(1),
            pl.BlockSpec((rows, columns, pixels), whole),
            pl.BlockSpec((1, 1, pixels), whole),
        ],
        out_specs=[pl.BlockSpec((rows, columns, pixels), whole)] * 2,
    )
    return pl.pallas_call(
        project_kernel,
        grid_spec=grid_spec,
        out_shape=[jax.ShapeDtypeStruct(measured.shape, jnp.float32)] * 2,
        compiler_params=pltpu.CompilerParams(vmem_limit_bytes=VMEM),
        name="project",
    )(place, start, weights, copies, copies, measured, dark_level.reshape(1, 1, pixels))


def gathered_pairs(operator_rows):
    held, pixels = operator_rows.shape
    if held == 2 * pixels:
        return lax.all_gather(operator_rows.T, "lenslet", axis=0)
    every = lax.all_gather(operator_rows, "lenslet", axis=0, tiled=True)
    return every.reshape(-1, 2 * pixels, pixels).transpose(0, 2, 1)


IN_VMEM = pl.BlockSpec(memory_space=pltpu.VMEM)
IN_SMEM = pl.BlockSpec(memory_space=pltpu.SMEM)
IN_HBM = pl.BlockSpec(memory_space=pl.ANY)


def put_shifted(out_ref, depth, row, plane):
    columns, pixels = plane.shape
    wide = plane.astype(jnp.float32)
    col = lax.broadcasted_iota(jnp.int32, (columns, pixels), 0)
    depths = out_ref.shape[0] // SHIFTS
    for s in range(SHIFTS):
        step = s - REACH
        if step == 0:
            out_ref[s * depths + depth, row] = plane
            continue
        moved = pltpu.roll(wide, (-step) % columns, 0)
        inside = col < columns - step if step > 0 else col >= -step
        out_ref[s * depths + depth, row] = jnp.where(inside, moved, 0.0).astype(jnp.bfloat16)


def own_rows_kernel(volume_ref, out_ref, held, sems):
    depths, rows, _, _ = held.shape
    fetch = [pltpu.make_async_copy(volume_ref.at[d], held.at[d], sems.at[d]) for d in range(depths)]
    for copy in fetch:
        copy.start()
    for d, copy in enumerate(fetch):
        copy.wait()

        def step(r, carry, d=d):
            put_shifted(out_ref, d, r + REACH, held[d, r])
            return carry

        lax.fori_loop(0, rows, step, 0)


def edge_rows_kernel(above_ref, below_ref, old_ref, out_ref):
    depths, reach, _, _ = above_ref.shape
    rows = out_ref.shape[1] - 2 * reach

    def step(n, carry):
        d, r = n // reach, n % reach
        put_shifted(out_ref, d, r, above_ref[d, r])
        put_shifted(out_ref, d, r + rows + reach, below_ref[d, r])
        return carry

    lax.fori_loop(0, depths * reach, step, 0)


def own_rows(volume):
    depths, rows, columns, pixels = volume.shape
    shape = (SHIFTS * depths, rows + 2 * REACH, columns, pixels)
    return pl.pallas_call(
        own_rows_kernel,
        in_specs=[pl.BlockSpec(memory_space=pltpu.HBM)],
        scratch_shapes=[pltpu.VMEM(volume.shape, volume.dtype), pltpu.SemaphoreType.DMA((depths,))],
        out_specs=IN_VMEM,
        out_shape=pltpu.VMEM(shape, volume.dtype),
        compiler_params=pltpu.CompilerParams(vmem_limit_bytes=SMALL),
        name="own_rows",
    )(pltpu.with_memory_space_constraint(volume, pltpu.HBM))


def edge_rows(above, below, copies):
    return pl.pallas_call(
        edge_rows_kernel,
        in_specs=[IN_VMEM, IN_VMEM, IN_VMEM],
        out_specs=IN_VMEM,
        out_shape=pltpu.VMEM(copies.shape, copies.dtype),
        input_output_aliases={2: 0},
        compiler_params=pltpu.CompilerParams(vmem_limit_bytes=SMALL),
        name="edge_rows",
    )(above, below, copies)


def operator_spot(scalars, op, depths):
    end, depth = jnp.int32(0), jnp.int32(0)
    for d in range(depths):
        end = end + scalars[d]
        depth = depth + jnp.where(op >= end, 1, 0)
    at = depths + 2 * op
    return (scalars[at + 1] + REACH) * depths + depth, scalars[at] + REACH


def add_kernel(scalars, copies, *refs, plan, pieces, first, last):
    weights = refs[: 2 * pieces]
    refs = refs[2 * pieces :]
    if last:
        meas, dark, old, pred_out, ratio_out, acc, pred, ratio, sems = refs
    elif first:
        old, acc = None, refs[0]
    else:
        old, acc = refs
    depths = copies.shape[0] // SHIFTS
    columns, pixels = copies.shape[2:]
    lines = acc.shape[1]
    rows = lines // columns
    here, side = scalars[scalars.shape[0] - 2], scalars[scalars.shape[0] - 1]
    dims = (((1,), (1,)), ((), ()))
    jobs = []
    for n, (hops, other, kind) in enumerate(plan):
        shard = ((here + (16 - 4 * hops)) % 16) ^ (2 * other)
        half = n if kind is None else side ^ kind
        spots = []
        for core in range(2):
            for which in range(2):
                spots.append(operator_spot(scalars, 2 * (shard ^ core) + which, depths))
        jobs.append((n, half, spots))

    for t in range(rows // TILE):
        m = slice(t * TILE * columns, (t + 1) * TILE * columns)
        for n, half, spots in jobs:
            total = None
            for j, (copy, row) in enumerate(spots):
                w_ref = weights[2 * n + j // 2]
                w = w_ref[0] if w_ref.shape[0] == 1 else w_ref[n]
                w = w[:, pixels * (j % 2) : pixels * (j % 2 + 1)]
                slab = copies[copy, pl.ds(row + t * TILE, TILE)].reshape(TILE * columns, pixels)
                part = lax.dot_general(slab, w, dims, preferred_element_type=jnp.float32)
                total = part if total is None else total + part
            if first:
                acc[half, m] = total
            elif last and n == 0:
                acc[half, m] = old[half, m] + total
                acc[1 - half, m] = old[1 - half, m]
            elif last:
                acc[half, m] = acc[half, m] + total
            else:
                acc[half, m] = acc[half, m] + total if n else old[half, m] + total
        if last:
            r = slice(t * TILE, (t + 1) * TILE)
            full = jnp.concatenate([acc[0, m], acc[1, m]], axis=1).reshape(TILE, columns, pixels)
            pred[r] = full
            ratio[r] = meas[r] / (full + dark[...].reshape(1, 1, pixels))
            for q, (src, dst) in enumerate(((pred, pred_out), (ratio, ratio_out))):
                pltpu.make_async_copy(src.at[r], dst.at[r], sems.at[2 * t + q]).start()
    if last:
        for t in range(rows // TILE):
            r = slice(t * TILE, (t + 1) * TILE)
            for q, (src, dst) in enumerate(((pred, pred_out), (ratio, ratio_out))):
                pltpu.make_async_copy(src.at[r], dst.at[r], sems.at[2 * t + q]).wait()


def add_pieces(scalars, copies, weights, plan, acc, final=None):
    columns, pixels = copies.shape[2:]
    rows = copies.shape[1] - 2 * REACH
    lines, part = rows * columns, pixels // 2
    pieces = len(plan)
    operands = [scalars, copies, *weights]
    shape = (2, lines, part)
    scratch, params = [], {}
    alias = {}
    if final is not None:
        operands += [*final, acc]
        full = final[0].shape
        out_shape = [jax.ShapeDtypeStruct(full, jnp.float32)] * 2
        out_specs = [IN_HBM] * 2
        scratch = [pltpu.VMEM(shape, jnp.float32), pltpu.VMEM(full, jnp.float32), pltpu.VMEM(full, jnp.float32)]
        scratch.append(pltpu.SemaphoreType.DMA((2 * (rows // TILE),)))
    else:
        out_shape, out_specs = pltpu.VMEM(shape, jnp.float32), IN_VMEM
        if acc is not None:
            alias = {len(operands): 0}
            operands.append(acc)
    flops = 2 * lines * 4 * pixels * part * pieces
    return pl.pallas_call(
        functools.partial(add_kernel, plan=plan, pieces=pieces, first=acc is None, last=final is not None),
        in_specs=[IN_SMEM] + [IN_VMEM] * (len(operands) - 1),
        out_specs=out_specs,
        out_shape=out_shape,
        scratch_shapes=scratch,
        input_output_aliases=alias,
        cost_estimate=pl.CostEstimate(flops=flops, bytes_accessed=pieces * 1024 * 1024, transcendentals=0),
        compiler_params=pltpu.CompilerParams(vmem_limit_bytes=SMALL),
        name="add_pieces",
    )(*operands)


def placements(offset_counts, offset_table):
    depths = offset_counts.shape[0]
    planes = jnp.arange(depths, dtype=jnp.int32)
    ends = jnp.sum(jnp.where(planes[None, :] <= planes[:, None], offset_counts[None, :], 0), axis=1)
    positions = jnp.arange(offset_table.shape[0], dtype=jnp.int32)
    depth_of = jnp.sum((positions[:, None] >= ends[None, :]).astype(jnp.int32), axis=1)
    return (offset_table[:, 1] + REACH) * depths + depth_of, offset_table[:, 0] + REACH


def exchanged(volume, measured, operator_rows, offset_counts, offset_table, dark_level):
    depths, rows, columns, pixels = volume.shape
    part = pixels // 2
    side = lax.axis_index("frames")
    here = lax.axis_index("lenslet")
    count = lax.axis_size("lenslet")
    scalars = jnp.concatenate([offset_counts, offset_table.reshape(-1), jnp.stack([here, side])])

    up = [(i, (i + 4) % count) for i in range(count)]
    beside = [(i, i ^ 2) for i in range(count)]
    twin = [(i, i ^ 1) for i in range(count)]
    along_z = lambda v: lax.ppermute(v, "lenslet", up)
    along_y = lambda v: lax.ppermute(v, "lenslet", beside)
    to_core = lambda v: lax.ppermute(v, "lenslet", twin)
    along_x = lambda v: lax.ppermute(v, "frames", [(0, 1), (1, 0)])

    own = operator_rows.T.reshape(2, part, 2 * pixels)
    own_a = lax.dynamic_index_in_dim(own, side, 0)
    own_b = lax.dynamic_index_in_dim(own, 1 - side, 0)
    both = lambda *pieces: [w for piece in pieces for w in (piece, to_core(piece))]

    tied = lax.optimization_barrier
    a, b = 0, 1
    own_a, own_b, volume = tied((own_a, own_b, volume))
    t1a, y0a = along_z(own_a), along_y(own_a)
    above = passed_along(volume[:, rows - REACH :], "lenslet", 1)
    below = passed_along(volume[:, :REACH], "lenslet", -1)
    own_c = to_core(own)
    volume, scalars, own_b = tied((volume, scalars, own_b))
    copies = own_rows(volume)
    t1a, y0a, copies = tied((t1a, y0a, copies))
    t2a, y1a, y0b = along_z(t1a), along_y(t1a), along_x(y0a)
    r0 = both(t1a, y0a)
    copies = edge_rows(above, below, copies)
    acc = add_pieces(scalars, copies, [own, own_c, own, own_c], [(0, 0, None), (0, 0, None)], None)
    acc = add_pieces(scalars, copies, r0, [(1, 0, a), (0, 1, a)], acc)
    t2a, y1a, y0b, acc = tied((t2a, y1a, y0b, acc))
    t3a, y2a, y1b = along_z(t2a), along_y(t2a), along_x(y1a)
    r1 = both(t2a, y1a, y0b)
    acc = add_pieces(scalars, copies, r1, [(2, 0, a), (1, 1, a), (0, 1, b)], acc)
    t3a, y2a, y1b, acc = tied((t3a, y2a, y1b, acc))
    t1b, y3a, t2b = along_z(own_b), along_y(t3a), along_x(t2a)
    r2 = both(t3a, y2a, y1b)
    acc = add_pieces(scalars, copies, r2, [(3, 0, a), (2, 1, a), (1, 1, b)], acc)
    t1b, y3a, t2b, acc = tied((t1b, y3a, t2b, acc))
    t3b, y2b, y3b = along_z(t2b), along_y(t2b), along_x(y3a)
    r3 = both(t1b, y3a, t2b)
    acc = add_pieces(scalars, copies, r3, [(1, 0, b), (3, 1, a), (2, 0, b)], acc)
    t3b, y2b, y3b, acc = tied((t3b, y2b, y3b, acc))
    r4 = both(t3b, y2b, y3b)
    final = (measured, dark_level.reshape(1, pixels))
    return tuple(add_pieces(scalars, copies, r4, [(3, 0, b), (2, 1, b), (3, 1, b)], acc, final))


def gathered(volume, measured, operator_rows, offset_counts, offset_table, dark_level):
    depths, rows, columns, pixels = volume.shape
    place, start = placements(offset_counts, offset_table)
    weights = gathered_pairs(operator_rows)
    above = passed_along(volume[:, rows - REACH :], "lenslet", 1)
    below = passed_along(volume[:, :REACH], "lenslet", -1)
    copies = shifted_copies(volume, above, below)
    copies = copies.reshape(SHIFTS * depths, rows + 2 * REACH, columns, pixels)
    return tuple(project(copies, weights, place, start, measured, dark_level))


def body(volume, measured, operator_rows, offset_counts, offset_table, dark_level):
    pairs = operator_rows.shape[0] == 2 * operator_rows.shape[1]
    known = lax.axis_size("lenslet") == 16 and lax.axis_size("frames") == 2
    form = exchanged if pairs and known else gathered
    return form(volume, measured, operator_rows, offset_counts, offset_table, dark_level)


def solution(mesh):
    placed = (
        P("frames", "lenslet", None, None),
        P(("frames", "lenslet"), None, None),
        P("lenslet", None),
        P(),
        P(),
        P(),
    )
    return jax.shard_map(
        body,
        mesh=mesh,
        in_specs=placed,
        out_specs=(P(("frames", "lenslet"), None, None), P(("frames", "lenslet"), None, None)),
        check_vma=False,
    )
```

```python
import functools

import jax
import jax.numpy as jnp
from jax import lax
from jax.experimental import pallas as pl
from jax.experimental.pallas import tpu as pltpu
from jax.sharding import PartitionSpec as P

REACH = 2
SHIFTS = 2 * REACH + 1
VMEM = 60 * 1024 * 1024
SMALL = 12 * 1024 * 1024
TILE = 8
LANES = 128
GROUP = 16
EDGE = 32
MINE, THEIRS, BOTH = (0,), (1,), (0, 1)


def passed_along(block, axis, distance):
    devices = range(lax.axis_size(axis))
    route = [(i - distance, i) for i in devices if i - distance in devices]
    return lax.ppermute(block, axis, route)


def shift_kernel(own_ref, above_ref, below_ref, out_ref):
    rows, columns, pixels = own_ref.shape[1:]
    col = lax.broadcasted_iota(jnp.int32, (columns, pixels), 0)

    def put(row, plane):
        wide = plane.astype(jnp.float32)
        for s in range(SHIFTS):
            step = s - REACH
            if step == 0:
                moved = wide
            else:
                moved = pltpu.roll(wide, (-step) % columns, 0)
                inside = col < columns - step if step > 0 else col >= -step
                moved = jnp.where(inside, moved, 0.0)
            out_ref[s, 0, row] = moved.astype(jnp.bfloat16)

    for r in range(REACH):
        put(r, above_ref[0, r])
        put(rows + REACH + r, below_ref[0, r])

    def step(r, carry):
        put(r + REACH, own_ref[0, r])
        return carry

    lax.fori_loop(0, rows, step, 0)


def shifted_copies(volume, above, below):
    depths, rows, columns, pixels = volume.shape
    ext = rows + 2 * REACH
    return pl.pallas_call(
        shift_kernel,
        grid=(depths,),
        in_specs=[
            pl.BlockSpec((1, rows, columns, pixels), lambda d: (d, 0, 0, 0)),
            pl.BlockSpec((1, REACH, columns, pixels), lambda d: (d, 0, 0, 0)),
            pl.BlockSpec((1, REACH, columns, pixels), lambda d: (d, 0, 0, 0)),
        ],
        out_specs=pl.BlockSpec((SHIFTS, 1, ext, columns, pixels), lambda d: (0, d, 0, 0, 0)),
        out_shape=jax.ShapeDtypeStruct((SHIFTS, depths, ext, columns, pixels), jnp.bfloat16),
        compiler_params=pltpu.CompilerParams(vmem_limit_bytes=VMEM),
        name="shifted_copies",
    )(volume, above, below)


def project_kernel(place_ref, start_ref, w_ref, even_ref, odd_ref, meas_ref, dark_ref, pred_ref, ratio_ref):
    i = pl.program_id(0)
    rows, columns, pixels = pred_ref.shape
    dims = (((1,), (1,)), ((), ()))
    a = even_ref[0].reshape(rows * columns, pixels)
    b = odd_ref[0].reshape(rows * columns, pixels)
    w = w_ref[0]
    part = lax.dot_general(a, w[:, :pixels], dims, preferred_element_type=jnp.float32)
    part = part + lax.dot_general(b, w[:, pixels:], dims, preferred_element_type=jnp.float32)
    part = part.reshape(rows, columns, pixels)

    @pl.when(i == 0)
    def _():
        pred_ref[...] = part

    @pl.when(i > 0)
    def _():
        pred_ref[...] = pred_ref[...] + part

    @pl.when(i == pl.num_programs(0) - 1)
    def _():
        ratio_ref[...] = meas_ref[...] / (pred_ref[...] + dark_ref[...])


def project(copies, weights, place, start, measured, dark_level):
    rows, columns, pixels = measured.shape
    shards, _, pair = weights.shape
    whole = lambda i, *_: (0, 0, 0)

    def slab(which):
        return pl.BlockSpec(
            (pl.Element(1), pl.Element(rows), pl.Element(columns), pl.Element(pixels)),
            lambda i, place_ref, start_ref: (
                place_ref[jnp.minimum(2 * i + which, 2 * shards - 1)],
                start_ref[jnp.minimum(2 * i + which, 2 * shards - 1)],
                0,
                0,
            ),
        )

    grid_spec = pltpu.PrefetchScalarGridSpec(
        num_scalar_prefetch=2,
        grid=(shards,),
        in_specs=[
            pl.BlockSpec((1, pixels, pair), lambda i, *_: (i, 0, 0)),
            slab(0),
            slab(1),
            pl.BlockSpec((rows, columns, pixels), whole),
            pl.BlockSpec((1, 1, pixels), whole),
        ],
        out_specs=[pl.BlockSpec((rows, columns, pixels), whole)] * 2,
    )
    return pl.pallas_call(
        project_kernel,
        grid_spec=grid_spec,
        out_shape=[jax.ShapeDtypeStruct(measured.shape, jnp.float32)] * 2,
        compiler_params=pltpu.CompilerParams(vmem_limit_bytes=VMEM),
        name="project",
    )(place, start, weights, copies, copies, measured, dark_level.reshape(1, 1, pixels))


def gathered_pairs(operator_rows):
    held, pixels = operator_rows.shape
    if held == 2 * pixels:
        return lax.all_gather(operator_rows.T, "lenslet", axis=0)
    every = lax.all_gather(operator_rows, "lenslet", axis=0, tiled=True)
    return every.reshape(-1, 2 * pixels, pixels).transpose(0, 2, 1)


IN_VMEM = pl.BlockSpec(memory_space=pltpu.VMEM)
IN_SMEM = pl.BlockSpec(memory_space=pltpu.SMEM)
IN_HBM = pl.BlockSpec(memory_space=pl.ANY)


def put_shifted(out_ref, depth, row, plane):
    columns, pixels = plane.shape
    wide = plane.astype(jnp.float32)
    col = lax.broadcasted_iota(jnp.int32, (columns, pixels), 0)
    depths = out_ref.shape[0] // SHIFTS
    for s in range(SHIFTS):
        step = s - REACH
        if step == 0:
            out_ref[s * depths + depth, row] = plane
            continue
        moved = pltpu.roll(wide, (-step) % columns, 0)
        inside = col < columns - step if step > 0 else col >= -step
        out_ref[s * depths + depth, row] = jnp.where(inside, moved, 0.0).astype(jnp.bfloat16)


def own_rows_kernel(volume_ref, out_ref, held, sems):
    depths, rows, _, _ = held.shape
    fetch = [pltpu.make_async_copy(volume_ref.at[d], held.at[d], sems.at[d]) for d in range(depths)]
    for copy in fetch:
        copy.start()
    for d, copy in enumerate(fetch):
        copy.wait()

        def step(r, carry, d=d):
            put_shifted(out_ref, d, r + REACH, held[d, r])
            return carry

        lax.fori_loop(0, rows, step, 0)


def edge_rows_kernel(above_ref, below_ref, old_ref, out_ref):
    depths = out_ref.shape[0] // SHIFTS
    rows, columns, pixels = out_ref.shape[1] - 2 * REACH, out_ref.shape[2], out_ref.shape[3]
    tail = pixels - above_ref.shape[1]
    pieces = columns // EDGE
    for k in range(depths * REACH):
        for packed, begin in ((above_ref, 0), (below_ref, rows + REACH)):
            left = [packed[:EDGE, tail * (k * pieces + j) : tail * (k * pieces + j + 1)] for j in range(pieces)]
            plane = packed[EDGE + k * columns : EDGE + (k + 1) * columns]
            plane = jnp.concatenate([plane, jnp.concatenate(left, axis=0)], axis=1)
            put_shifted(out_ref, k // REACH, begin + k % REACH, plane)


def own_rows(volume):
    depths, rows, columns, pixels = volume.shape
    shape = (SHIFTS * depths, rows + 2 * REACH, columns, pixels)
    return pl.pallas_call(
        own_rows_kernel,
        in_specs=[pl.BlockSpec(memory_space=pltpu.HBM)],
        scratch_shapes=[pltpu.VMEM(volume.shape, volume.dtype), pltpu.SemaphoreType.DMA((depths,))],
        out_specs=IN_VMEM,
        out_shape=pltpu.VMEM(shape, volume.dtype),
        compiler_params=pltpu.CompilerParams(vmem_limit_bytes=SMALL),
        name="own_rows",
    )(pltpu.with_memory_space_constraint(volume, pltpu.HBM))


def edge_rows(above, below, copies):
    return pl.pallas_call(
        edge_rows_kernel,
        in_specs=[IN_VMEM, IN_VMEM, IN_VMEM],
        out_specs=IN_VMEM,
        out_shape=pltpu.VMEM(copies.shape, copies.dtype),
        input_output_aliases={2: 0},
        compiler_params=pltpu.CompilerParams(vmem_limit_bytes=SMALL),
        name="edge_rows",
    )(above, below, copies)


def pack_pieces_kernel(scalars, own_ref, a_ref, b_ref):
    _, part, pair = own_ref.shape
    pixels = pair // 2
    wide = pixels // LANES * LANES
    side = scalars[scalars.shape[0] - 1]
    for out_ref, half in ((a_ref, side), (b_ref, 1 - side)):
        w = own_ref[half]
        out_ref[GROUP:, :wide] = w[:, :wide]
        out_ref[GROUP:, wide:] = w[:, pixels : pixels + wide]
        left = jnp.concatenate([w[:, wide:pixels], w[:, pixels + wide :]], axis=1)
        tail = left.shape[1]
        groups = -(-part // GROUP)
        left = jnp.concatenate([left, jnp.zeros((groups * GROUP - part, tail), left.dtype)], axis=0)
        cut = [left[GROUP * n : GROUP * (n + 1)] for n in range(groups)]
        cut.append(jnp.zeros((GROUP, 2 * wide - groups * tail), left.dtype))
        out_ref[:GROUP] = jnp.concatenate(cut, axis=1)


def pack_pieces(scalars, own):
    _, part, pair = own.shape
    packed = jax.ShapeDtypeStruct((GROUP + part, pair // 2 // LANES * LANES * 2), own.dtype)
    return pl.pallas_call(
        pack_pieces_kernel,
        in_specs=[IN_SMEM, IN_VMEM],
        out_specs=[IN_VMEM] * 2,
        out_shape=[pltpu.VMEM(packed.shape, packed.dtype)] * 2,
        compiler_params=pltpu.CompilerParams(vmem_limit_bytes=SMALL),
        name="pack_pieces",
    )(scalars, own)


def unpacked(w_ref, n, which, part, pixels):
    if len(w_ref.shape) == 3:
        return w_ref[n, :, pixels * which : pixels * (which + 1)]
    wide = w_ref.shape[1] // 2
    tail = pixels - wide
    groups = -(-part // GROUP)
    first = [w_ref[:GROUP, 2 * tail * k + tail * which : 2 * tail * k + tail * (which + 1)] for k in range(groups)]
    left = jnp.concatenate(first, axis=0)[:part]
    return jnp.concatenate([w_ref[GROUP:, wide * which : wide * (which + 1)], left], axis=1)


def pack_rows_kernel(volume_ref, last_ref, first_ref, held, sems):
    depths, rows, columns, pixels = volume_ref.shape
    wide = pixels // LANES * LANES
    begins = (rows - REACH, 0)
    fetch = [
        pltpu.make_async_copy(volume_ref.at[:, pl.ds(begin, REACH)], held.at[n], sems.at[n])
        for n, begin in enumerate(begins)
    ]
    for copy in fetch:
        copy.start()
    for n, out_ref in enumerate((last_ref, first_ref)):
        fetch[n].wait()
        cut = []
        for k in range(depths * REACH):
            plane = held[n, k // REACH, k % REACH]
            out_ref[EDGE + k * columns : EDGE + (k + 1) * columns] = plane[:, :wide]
            cut += [plane[EDGE * j : EDGE * (j + 1), wide:] for j in range(columns // EDGE)]
        cut.append(jnp.zeros((EDGE, wide - len(cut) * (pixels - wide)), volume_ref.dtype))
        out_ref[:EDGE] = jnp.concatenate(cut, axis=1)


def pack_rows(volume):
    depths, _, columns, pixels = volume.shape
    shape = (EDGE + depths * REACH * columns, pixels // LANES * LANES)
    return pl.pallas_call(
        pack_rows_kernel,
        in_specs=[pl.BlockSpec(memory_space=pltpu.HBM)],
        out_specs=[IN_VMEM] * 2,
        out_shape=[pltpu.VMEM(shape, volume.dtype)] * 2,
        scratch_shapes=[
            pltpu.VMEM((2, depths, REACH, columns, pixels), volume.dtype),
            pltpu.SemaphoreType.DMA((2,)),
        ],
        compiler_params=pltpu.CompilerParams(vmem_limit_bytes=SMALL),
        name="pack_rows",
    )(pltpu.with_memory_space_constraint(volume, pltpu.HBM))


def operator_spot(scalars, op, depths):
    end, depth = jnp.int32(0), jnp.int32(0)
    for d in range(depths):
        end = end + scalars[d]
        depth = depth + jnp.where(op >= end, 1, 0)
    at = depths + 2 * op
    return (scalars[at + 1] + REACH) * depths + depth, scalars[at] + REACH


def add_kernel(scalars, copies, *refs, plan, pieces, first, last):
    weights = refs[:pieces]
    refs = refs[pieces:]
    if last:
        meas, dark, old, pred_out, ratio_out, acc, pred, ratio, sems = refs
    elif first:
        old, acc = None, refs[0]
    else:
        old, acc = refs
    depths = copies.shape[0] // SHIFTS
    columns, pixels = copies.shape[2:]
    lines = acc.shape[1]
    rows = lines // columns
    here, side = scalars[scalars.shape[0] - 2], scalars[scalars.shape[0] - 1]
    dims = (((1,), (1,)), ((), ()))
    jobs, at = [], 0
    for n, (hops, other, kind, cores) in enumerate(plan):
        shard = ((here + (16 - 4 * hops)) % 16) ^ (2 * other)
        half = n if kind is None else side ^ kind
        products = []
        for core in cores:
            for which in range(2):
                copy, row = operator_spot(scalars, 2 * (shard ^ core) + which, depths)
                products.append((at, which, copy, row))
            at += 1
        jobs.append((n, half, products))

    for t in range(rows // TILE):
        m = slice(t * TILE * columns, (t + 1) * TILE * columns)
        for n, half, products in jobs:
            total = None
            for at, which, copy, row in products:
                w = unpacked(weights[at], n, which, acc.shape[2], pixels)
                slab = copies[copy, pl.ds(row + t * TILE, TILE)].reshape(TILE * columns, pixels)
                part = lax.dot_general(slab, w, dims, preferred_element_type=jnp.float32)
                total = part if total is None else total + part
            if first:
                acc[half, m] = total
            elif last and n == 0:
                acc[half, m] = old[half, m] + total
                acc[1 - half, m] = old[1 - half, m]
            elif last:
                acc[half, m] = acc[half, m] + total
            else:
                acc[half, m] = acc[half, m] + total if n else old[half, m] + total
        if last:
            r = slice(t * TILE, (t + 1) * TILE)
            full = jnp.concatenate([acc[0, m], acc[1, m]], axis=1).reshape(TILE, columns, pixels)
            pred[r] = full
            ratio[r] = meas[r] / (full + dark[...].reshape(1, 1, pixels))
            for q, (src, dst) in enumerate(((pred, pred_out), (ratio, ratio_out))):
                pltpu.make_async_copy(src.at[r], dst.at[r], sems.at[2 * t + q]).start()
    if last:
        for t in range(rows // TILE):
            r = slice(t * TILE, (t + 1) * TILE)
            for q, (src, dst) in enumerate(((pred, pred_out), (ratio, ratio_out))):
                pltpu.make_async_copy(src.at[r], dst.at[r], sems.at[2 * t + q]).wait()


def add_pieces(scalars, copies, weights, plan, acc, final=None):
    columns, pixels = copies.shape[2:]
    rows = copies.shape[1] - 2 * REACH
    lines, part = rows * columns, pixels // 2
    pieces = len(weights)
    operands = [scalars, copies, *weights]
    shape = (2, lines, part)
    scratch, params = [], {}
    alias = {}
    if final is not None:
        operands += [*final, acc]
        full = final[0].shape
        out_shape = [jax.ShapeDtypeStruct(full, jnp.float32)] * 2
        out_specs = [IN_HBM] * 2
        scratch = [pltpu.VMEM(shape, jnp.float32), pltpu.VMEM(full, jnp.float32), pltpu.VMEM(full, jnp.float32)]
        scratch.append(pltpu.SemaphoreType.DMA((2 * (rows // TILE),)))
    else:
        out_shape, out_specs = pltpu.VMEM(shape, jnp.float32), IN_VMEM
        if acc is not None:
            alias = {len(operands): 0}
            operands.append(acc)
    flops = 2 * lines * 4 * pixels * part * pieces
    return pl.pallas_call(
        functools.partial(add_kernel, plan=plan, pieces=pieces, first=acc is None, last=final is not None),
        in_specs=[IN_SMEM] + [IN_VMEM] * (len(operands) - 1),
        out_specs=out_specs,
        out_shape=out_shape,
        scratch_shapes=scratch,
        input_output_aliases=alias,
        cost_estimate=pl.CostEstimate(flops=flops, bytes_accessed=pieces * 1024 * 1024, transcendentals=0),
        compiler_params=pltpu.CompilerParams(vmem_limit_bytes=SMALL),
        name="add_pieces",
    )(*operands)


def placements(offset_counts, offset_table):
    depths = offset_counts.shape[0]
    planes = jnp.arange(depths, dtype=jnp.int32)
    ends = jnp.sum(jnp.where(planes[None, :] <= planes[:, None], offset_counts[None, :], 0), axis=1)
    positions = jnp.arange(offset_table.shape[0], dtype=jnp.int32)
    depth_of = jnp.sum((positions[:, None] >= ends[None, :]).astype(jnp.int32), axis=1)
    return (offset_table[:, 1] + REACH) * depths + depth_of, offset_table[:, 0] + REACH


def exchanged(volume, measured, operator_rows, offset_counts, offset_table, dark_level):
    depths, rows, columns, pixels = volume.shape
    part = pixels // 2
    side = lax.axis_index("frames")
    here = lax.axis_index("lenslet")
    count = lax.axis_size("lenslet")
    scalars = jnp.concatenate([offset_counts, offset_table.reshape(-1), jnp.stack([here, side])])

    up = [(i, (i + 4) % count) for i in range(count)]
    beside = [(i, i ^ 2) for i in range(count)]
    twin = [(i, i ^ 1) for i in range(count)]
    along_z = lambda v: lax.ppermute(v, "lenslet", up)
    along_y = lambda v: lax.ppermute(v, "lenslet", beside)
    to_core = lambda v: lax.ppermute(v, "lenslet", twin)
    along_x = lambda v: lax.ppermute(v, "frames", [(0, 1), (1, 0)])

    own = operator_rows.T.reshape(2, part, 2 * pixels)
    both = lambda *pieces: [w for piece in pieces for w in (piece, to_core(piece))]

    tied = lax.optimization_barrier
    a, b = 0, 1
    scalars, own = tied((scalars, own))
    own_a, own_b = pack_pieces(scalars, own)
    t1a, y0a = along_z(own_a), along_y(own_a)
    own_c = to_core(own)
    last_rows, first_rows = pack_rows(volume)
    above, below = passed_along(last_rows, "lenslet", 1), passed_along(first_rows, "lenslet", -1)
    copies = own_rows(volume)
    t1a, y0a, copies = tied((t1a, y0a, copies))
    t2a, y1a, y0b = along_z(t1a), along_y(t1a), along_x(y0a)
    r0 = both(t1a, y0a)
    copies = edge_rows(above, below, copies)
    acc = add_pieces(scalars, copies, [own, own_c, own, own_c], [(0, 0, None, BOTH), (0, 0, None, BOTH)], None)
    acc = add_pieces(scalars, copies, r0, [(1, 0, a, BOTH), (0, 1, a, BOTH)], acc)
    t2a, y1a, y0b, acc = tied((t2a, y1a, y0b, acc))
    t3a, y2a, y1b = along_z(t2a), along_y(t2a), along_x(y1a)
    r1 = both(t2a, y1a, y0b)
    acc = add_pieces(scalars, copies, r1, [(2, 0, a, BOTH), (1, 1, a, BOTH), (0, 1, b, BOTH)], acc)
    t3a, y2a, y1b, acc = tied((t3a, y2a, y1b, acc))
    t1b, y3a, t2b = along_z(own_b), along_y(t3a), along_x(t2a)
    r2 = both(t3a, y2a, y1b)
    acc = add_pieces(scalars, copies, r2, [(3, 0, a, BOTH), (2, 1, a, BOTH), (1, 1, b, BOTH)], acc)
    t2b, y3a, t1b, acc = tied((t2b, y3a, t1b, acc))
    t3b, y2b, y3b = along_z(t2b), along_y(t2b), along_x(y3a)
    r3 = both(t1b, y3a, t2b)
    acc = add_pieces(scalars, copies, r3, [(1, 0, b, BOTH), (3, 1, a, BOTH), (2, 0, b, BOTH)], acc)
    t3b, acc = tied((t3b, acc))
    y2b, acc = tied((y2b, acc))
    y3b, acc = tied((y3b, acc))
    r4 = both(t3b, y2b, y3b)
    acc = add_pieces(scalars, copies, r4[0::2], [(3, 0, b, MINE), (2, 1, b, MINE), (3, 1, b, MINE)], acc)
    final = (measured, dark_level.reshape(1, pixels))
    plan = [(3, 0, b, THEIRS), (2, 1, b, THEIRS), (3, 1, b, THEIRS)]
    return tuple(add_pieces(scalars, copies, r4[1::2], plan, acc, final))


def gathered(volume, measured, operator_rows, offset_counts, offset_table, dark_level):
    depths, rows, columns, pixels = volume.shape
    place, start = placements(offset_counts, offset_table)
    weights = gathered_pairs(operator_rows)
    above = passed_along(volume[:, rows - REACH :], "lenslet", 1)
    below = passed_along(volume[:, :REACH], "lenslet", -1)
    copies = shifted_copies(volume, above, below)
    copies = copies.reshape(SHIFTS * depths, rows + 2 * REACH, columns, pixels)
    return tuple(project(copies, weights, place, start, measured, dark_level))


def body(volume, measured, operator_rows, offset_counts, offset_table, dark_level):
    pairs = operator_rows.shape[0] == 2 * operator_rows.shape[1]
    known = lax.axis_size("lenslet") == 16 and lax.axis_size("frames") == 2
    form = exchanged if pairs and known else gathered
    return form(volume, measured, operator_rows, offset_counts, offset_table, dark_level)


def solution(mesh):
    placed = (
        P("frames", "lenslet", None, None),
        P(("frames", "lenslet"), None, None),
        P("lenslet", None),
        P(),
        P(),
        P(),
    )
    return jax.shard_map(
        body,
        mesh=mesh,
        in_specs=placed,
        out_specs=(P(("frames", "lenslet"), None, None), P(("frames", "lenslet"), None, None)),
        check_vma=False,
    )
```

```python
import functools

import jax
import jax.numpy as jnp
from jax import lax
from jax.experimental import pallas as pl
from jax.experimental.pallas import tpu as pltpu
from jax.sharding import PartitionSpec as P

REACH = 2
SHIFTS = 2 * REACH + 1
VMEM = 60 * 1024 * 1024
SMALL = 12 * 1024 * 1024
TILE = 8
LANES = 128
GROUP = 16
EDGE = 32
MINE, THEIRS, BOTH = (0,), (1,), (0, 1)


def passed_along(block, axis, distance):
    devices = range(lax.axis_size(axis))
    route = [(i - distance, i) for i in devices if i - distance in devices]
    return lax.ppermute(block, axis, route)


def shift_kernel(own_ref, above_ref, below_ref, out_ref):
    rows, columns, pixels = own_ref.shape[1:]
    col = lax.broadcasted_iota(jnp.int32, (columns, pixels), 0)

    def put(row, plane):
        wide = plane.astype(jnp.float32)
        for s in range(SHIFTS):
            step = s - REACH
            if step == 0:
                moved = wide
            else:
                moved = pltpu.roll(wide, (-step) % columns, 0)
                inside = col < columns - step if step > 0 else col >= -step
                moved = jnp.where(inside, moved, 0.0)
            out_ref[s, 0, row] = moved.astype(jnp.bfloat16)

    for r in range(REACH):
        put(r, above_ref[0, r])
        put(rows + REACH + r, below_ref[0, r])

    def step(r, carry):
        put(r + REACH, own_ref[0, r])
        return carry

    lax.fori_loop(0, rows, step, 0)


def shifted_copies(volume, above, below):
    depths, rows, columns, pixels = volume.shape
    ext = rows + 2 * REACH
    return pl.pallas_call(
        shift_kernel,
        grid=(depths,),
        in_specs=[
            pl.BlockSpec((1, rows, columns, pixels), lambda d: (d, 0, 0, 0)),
            pl.BlockSpec((1, REACH, columns, pixels), lambda d: (d, 0, 0, 0)),
            pl.BlockSpec((1, REACH, columns, pixels), lambda d: (d, 0, 0, 0)),
        ],
        out_specs=pl.BlockSpec((SHIFTS, 1, ext, columns, pixels), lambda d: (0, d, 0, 0, 0)),
        out_shape=jax.ShapeDtypeStruct((SHIFTS, depths, ext, columns, pixels), jnp.bfloat16),
        compiler_params=pltpu.CompilerParams(vmem_limit_bytes=VMEM),
        name="shifted_copies",
    )(volume, above, below)


def project_kernel(place_ref, start_ref, w_ref, even_ref, odd_ref, meas_ref, dark_ref, pred_ref, ratio_ref):
    i = pl.program_id(0)
    rows, columns, pixels = pred_ref.shape
    dims = (((1,), (1,)), ((), ()))
    a = even_ref[0].reshape(rows * columns, pixels)
    b = odd_ref[0].reshape(rows * columns, pixels)
    w = w_ref[0]
    part = lax.dot_general(a, w[:, :pixels], dims, preferred_element_type=jnp.float32)
    part = part + lax.dot_general(b, w[:, pixels:], dims, preferred_element_type=jnp.float32)
    part = part.reshape(rows, columns, pixels)

    @pl.when(i == 0)
    def _():
        pred_ref[...] = part

    @pl.when(i > 0)
    def _():
        pred_ref[...] = pred_ref[...] + part

    @pl.when(i == pl.num_programs(0) - 1)
    def _():
        ratio_ref[...] = meas_ref[...] / (pred_ref[...] + dark_ref[...])


def project(copies, weights, place, start, measured, dark_level):
    rows, columns, pixels = measured.shape
    shards, _, pair = weights.shape
    whole = lambda i, *_: (0, 0, 0)

    def slab(which):
        return pl.BlockSpec(
            (pl.Element(1), pl.Element(rows), pl.Element(columns), pl.Element(pixels)),
            lambda i, place_ref, start_ref: (
                place_ref[jnp.minimum(2 * i + which, 2 * shards - 1)],
                start_ref[jnp.minimum(2 * i + which, 2 * shards - 1)],
                0,
                0,
            ),
        )

    grid_spec = pltpu.PrefetchScalarGridSpec(
        num_scalar_prefetch=2,
        grid=(shards,),
        in_specs=[
            pl.BlockSpec((1, pixels, pair), lambda i, *_: (i, 0, 0)),
            slab(0),
            slab(1),
            pl.BlockSpec((rows, columns, pixels), whole),
            pl.BlockSpec((1, 1, pixels), whole),
        ],
        out_specs=[pl.BlockSpec((rows, columns, pixels), whole)] * 2,
    )
    return pl.pallas_call(
        project_kernel,
        grid_spec=grid_spec,
        out_shape=[jax.ShapeDtypeStruct(measured.shape, jnp.float32)] * 2,
        compiler_params=pltpu.CompilerParams(vmem_limit_bytes=VMEM),
        name="project",
    )(place, start, weights, copies, copies, measured, dark_level.reshape(1, 1, pixels))


def gathered_pairs(operator_rows):
    held, pixels = operator_rows.shape
    if held == 2 * pixels:
        return lax.all_gather(operator_rows.T, "lenslet", axis=0)
    every = lax.all_gather(operator_rows, "lenslet", axis=0, tiled=True)
    return every.reshape(-1, 2 * pixels, pixels).transpose(0, 2, 1)


IN_VMEM = pl.BlockSpec(memory_space=pltpu.VMEM)
IN_SMEM = pl.BlockSpec(memory_space=pltpu.SMEM)
IN_HBM = pl.BlockSpec(memory_space=pl.ANY)


def put_shifted(out_ref, depth, row, plane):
    columns, pixels = plane.shape
    wide = plane.astype(jnp.float32)
    col = lax.broadcasted_iota(jnp.int32, (columns, pixels), 0)
    depths = out_ref.shape[0] // SHIFTS
    for s in range(SHIFTS):
        step = s - REACH
        if step == 0:
            out_ref[s * depths + depth, row] = plane
            continue
        moved = pltpu.roll(wide, (-step) % columns, 0)
        inside = col < columns - step if step > 0 else col >= -step
        out_ref[s * depths + depth, row] = jnp.where(inside, moved, 0.0).astype(jnp.bfloat16)


def own_rows_kernel(volume_ref, out_ref, held, sems):
    depths, rows, _, _ = held.shape
    fetch = [pltpu.make_async_copy(volume_ref.at[d], held.at[d], sems.at[d]) for d in range(depths)]
    for copy in fetch:
        copy.start()
    for d, copy in enumerate(fetch):
        copy.wait()

        def step(r, carry, d=d):
            put_shifted(out_ref, d, r + REACH, held[d, r])
            return carry

        lax.fori_loop(0, rows, step, 0)


def edge_rows_kernel(above_ref, below_ref, old_ref, out_ref):
    depths = out_ref.shape[0] // SHIFTS
    rows, columns, pixels = out_ref.shape[1] - 2 * REACH, out_ref.shape[2], out_ref.shape[3]
    tail = pixels - above_ref.shape[1]
    pieces = columns // EDGE
    for k in range(depths * REACH):
        for packed, begin in ((above_ref, 0), (below_ref, rows + REACH)):
            left = [packed[:EDGE, tail * (k * pieces + j) : tail * (k * pieces + j + 1)] for j in range(pieces)]
            plane = packed[EDGE + k * columns : EDGE + (k + 1) * columns]
            plane = jnp.concatenate([plane, jnp.concatenate(left, axis=0)], axis=1)
            put_shifted(out_ref, k // REACH, begin + k % REACH, plane)


def own_rows(volume):
    depths, rows, columns, pixels = volume.shape
    shape = (SHIFTS * depths, rows + 2 * REACH, columns, pixels)
    return pl.pallas_call(
        own_rows_kernel,
        in_specs=[pl.BlockSpec(memory_space=pltpu.HBM)],
        scratch_shapes=[pltpu.VMEM(volume.shape, volume.dtype), pltpu.SemaphoreType.DMA((depths,))],
        out_specs=IN_VMEM,
        out_shape=pltpu.VMEM(shape, volume.dtype),
        compiler_params=pltpu.CompilerParams(vmem_limit_bytes=SMALL),
        name="own_rows",
    )(pltpu.with_memory_space_constraint(volume, pltpu.HBM))


def edge_rows(above, below, copies):
    return pl.pallas_call(
        edge_rows_kernel,
        in_specs=[IN_VMEM, IN_VMEM, IN_VMEM],
        out_specs=IN_VMEM,
        out_shape=pltpu.VMEM(copies.shape, copies.dtype),
        input_output_aliases={2: 0},
        compiler_params=pltpu.CompilerParams(vmem_limit_bytes=SMALL),
        name="edge_rows",
    )(above, below, copies)


def pack_pieces_kernel(side_ref, own_ref, a_ref, b_ref):
    _, part, pair = own_ref.shape
    pixels = pair // 2
    wide = pixels // LANES * LANES
    side = side_ref[0]
    for out_ref, half in ((a_ref, side), (b_ref, 1 - side)):
        w = own_ref[half]
        out_ref[GROUP:, :wide] = w[:, :wide]
        out_ref[GROUP:, wide:] = w[:, pixels : pixels + wide]
        left = jnp.concatenate([w[:, wide:pixels], w[:, pixels + wide :]], axis=1)
        tail = left.shape[1]
        groups = -(-part // GROUP)
        left = jnp.concatenate([left, jnp.zeros((groups * GROUP - part, tail), left.dtype)], axis=0)
        cut = [left[GROUP * n : GROUP * (n + 1)] for n in range(groups)]
        cut.append(jnp.zeros((GROUP, 2 * wide - groups * tail), left.dtype))
        out_ref[:GROUP] = jnp.concatenate(cut, axis=1)


def pack_pieces(side, own):
    _, part, pair = own.shape
    packed = jax.ShapeDtypeStruct((GROUP + part, pair // 2 // LANES * LANES * 2), own.dtype)
    return pl.pallas_call(
        pack_pieces_kernel,
        in_specs=[IN_SMEM, IN_VMEM],
        out_specs=[IN_VMEM] * 2,
        out_shape=[pltpu.VMEM(packed.shape, packed.dtype)] * 2,
        compiler_params=pltpu.CompilerParams(vmem_limit_bytes=SMALL),
        name="pack_pieces",
    )(side.reshape(1), own)


def unpacked(w_ref, n, which, part, pixels):
    if len(w_ref.shape) == 3:
        return w_ref[n, :, pixels * which : pixels * (which + 1)]
    wide = w_ref.shape[1] // 2
    tail = pixels - wide
    groups = -(-part // GROUP)
    first = [w_ref[:GROUP, 2 * tail * k + tail * which : 2 * tail * k + tail * (which + 1)] for k in range(groups)]
    left = jnp.concatenate(first, axis=0)[:part]
    return jnp.concatenate([w_ref[GROUP:, wide * which : wide * (which + 1)], left], axis=1)


def pack_rows_kernel(volume_ref, last_ref, first_ref, held, sems):
    depths, rows, columns, pixels = volume_ref.shape
    wide = pixels // LANES * LANES
    begins = (rows - REACH, 0)
    fetch = [
        pltpu.make_async_copy(volume_ref.at[:, pl.ds(begin, REACH)], held.at[n], sems.at[n])
        for n, begin in enumerate(begins)
    ]
    for copy in fetch:
        copy.start()
    for n, out_ref in enumerate((last_ref, first_ref)):
        fetch[n].wait()
        cut = []
        for k in range(depths * REACH):
            plane = held[n, k // REACH, k % REACH]
            out_ref[EDGE + k * columns : EDGE + (k + 1) * columns] = plane[:, :wide]
            cut += [plane[EDGE * j : EDGE * (j + 1), wide:] for j in range(columns // EDGE)]
        cut.append(jnp.zeros((EDGE, wide - len(cut) * (pixels - wide)), volume_ref.dtype))
        out_ref[:EDGE] = jnp.concatenate(cut, axis=1)


def pack_rows(volume):
    depths, _, columns, pixels = volume.shape
    shape = (EDGE + depths * REACH * columns, pixels // LANES * LANES)
    return pl.pallas_call(
        pack_rows_kernel,
        in_specs=[pl.BlockSpec(memory_space=pltpu.HBM)],
        out_specs=[IN_VMEM] * 2,
        out_shape=[pltpu.VMEM(shape, volume.dtype)] * 2,
        scratch_shapes=[
            pltpu.VMEM((2, depths, REACH, columns, pixels), volume.dtype),
            pltpu.SemaphoreType.DMA((2,)),
        ],
        compiler_params=pltpu.CompilerParams(vmem_limit_bytes=SMALL),
        name="pack_rows",
    )(pltpu.with_memory_space_constraint(volume, pltpu.HBM))


def operator_spot(scalars, op, depths):
    end, depth = jnp.int32(0), jnp.int32(0)
    for d in range(depths):
        end = end + scalars[d]
        depth = depth + jnp.where(op >= end, 1, 0)
    at = depths + 2 * op
    return (scalars[at + 1] + REACH) * depths + depth, scalars[at] + REACH


def add_kernel(scalars, copies, *refs, plan, pieces, first, last):
    weights = refs[:pieces]
    refs = refs[pieces:]
    if last:
        meas, dark, old, pred_out, ratio_out, acc, pred, ratio, sems = refs
    elif first:
        old, acc = None, refs[0]
    else:
        old, acc = refs
    depths = copies.shape[0] // SHIFTS
    columns, pixels = copies.shape[2:]
    lines = acc.shape[1]
    rows = lines // columns
    here, side = scalars[scalars.shape[0] - 2], scalars[scalars.shape[0] - 1]
    dims = (((1,), (1,)), ((), ()))
    jobs, at = [], 0
    for n, (hops, other, kind, cores) in enumerate(plan):
        shard = ((here + (16 - 4 * hops)) % 16) ^ (2 * other)
        half = n if kind is None else side ^ kind
        products = []
        for core in cores:
            for which in range(2):
                copy, row = operator_spot(scalars, 2 * (shard ^ core) + which, depths)
                products.append((at, which, copy, row))
            at += 1
        jobs.append((n, half, products))

    tile = 4 if last else TILE
    for t in range(rows // tile):
        m = slice(t * tile * columns, (t + 1) * tile * columns)
        for n, half, products in jobs:
            total = None
            for at, which, copy, row in products:
                w = unpacked(weights[at], n, which, acc.shape[2], pixels)
                slab = copies[copy, pl.ds(row + t * tile, tile)].reshape(tile * columns, pixels)
                part = lax.dot_general(slab, w, dims, preferred_element_type=jnp.float32)
                total = part if total is None else total + part
            if first:
                acc[half, m] = total
            elif last and n == 0:
                acc[half, m] = old[half, m] + total
                acc[1 - half, m] = old[1 - half, m]
            elif last:
                acc[half, m] = acc[half, m] + total
            else:
                acc[half, m] = acc[half, m] + total if n else old[half, m] + total
        if last:
            r = slice(t * tile, (t + 1) * tile)
            full = jnp.concatenate([acc[0, m], acc[1, m]], axis=1).reshape(tile, columns, pixels)
            pred[r] = full
            ratio[r] = meas[r] / (full + dark[...].reshape(1, 1, pixels))
            for q, (src, dst) in enumerate(((pred, pred_out), (ratio, ratio_out))):
                pltpu.make_async_copy(src.at[r], dst.at[r], sems.at[2 * t + q]).start()
    if last:
        for t in range(rows // tile):
            r = slice(t * tile, (t + 1) * tile)
            for q, (src, dst) in enumerate(((pred, pred_out), (ratio, ratio_out))):
                pltpu.make_async_copy(src.at[r], dst.at[r], sems.at[2 * t + q]).wait()


def add_pieces(scalars, copies, weights, plan, acc, final=None):
    columns, pixels = copies.shape[2:]
    rows = copies.shape[1] - 2 * REACH
    lines, part = rows * columns, pixels // 2
    pieces = len(weights)
    operands = [scalars, copies, *weights]
    shape = (2, lines, part)
    scratch, params = [], {}
    alias = {}
    if final is not None:
        operands += [*final, acc]
        full = final[0].shape
        out_shape = [jax.ShapeDtypeStruct(full, jnp.float32)] * 2
        out_specs = [IN_HBM] * 2
        scratch = [pltpu.VMEM(shape, jnp.float32), pltpu.VMEM(full, jnp.float32), pltpu.VMEM(full, jnp.float32)]
        scratch.append(pltpu.SemaphoreType.DMA((2 * (rows // 4),)))
    else:
        out_shape, out_specs = pltpu.VMEM(shape, jnp.float32), IN_VMEM
        if acc is not None:
            alias = {len(operands): 0}
            operands.append(acc)
    flops = 2 * lines * 4 * pixels * part * pieces
    return pl.pallas_call(
        functools.partial(add_kernel, plan=plan, pieces=pieces, first=acc is None, last=final is not None),
        in_specs=[IN_SMEM] + [IN_VMEM] * (len(operands) - 1),
        out_specs=out_specs,
        out_shape=out_shape,
        scratch_shapes=scratch,
        input_output_aliases=alias,
        cost_estimate=pl.CostEstimate(flops=flops, bytes_accessed=pieces * 1024 * 1024, transcendentals=0),
        compiler_params=pltpu.CompilerParams(vmem_limit_bytes=SMALL),
        name="add_pieces",
    )(*operands)


def placements(offset_counts, offset_table):
    depths = offset_counts.shape[0]
    planes = jnp.arange(depths, dtype=jnp.int32)
    ends = jnp.sum(jnp.where(planes[None, :] <= planes[:, None], offset_counts[None, :], 0), axis=1)
    positions = jnp.arange(offset_table.shape[0], dtype=jnp.int32)
    depth_of = jnp.sum((positions[:, None] >= ends[None, :]).astype(jnp.int32), axis=1)
    return (offset_table[:, 1] + REACH) * depths + depth_of, offset_table[:, 0] + REACH


def exchanged(volume, measured, operator_rows, offset_counts, offset_table, dark_level):
    depths, rows, columns, pixels = volume.shape
    part = pixels // 2
    side = lax.axis_index("frames")
    here = lax.axis_index("lenslet")
    count = lax.axis_size("lenslet")
    scalars = jnp.concatenate([offset_counts, offset_table.reshape(-1), jnp.stack([here, side])])

    up = [(i, (i + 4) % count) for i in range(count)]
    beside = [(i, i ^ 2) for i in range(count)]
    twin = [(i, i ^ 1) for i in range(count)]
    along_z = lambda v: lax.ppermute(v, "lenslet", up)
    along_y = lambda v: lax.ppermute(v, "lenslet", beside)
    to_core = lambda v: lax.ppermute(v, "lenslet", twin)
    along_x = lambda v: lax.ppermute(v, "frames", [(0, 1), (1, 0)])

    own = operator_rows.T.reshape(2, part, 2 * pixels)
    both = lambda *pieces: [w for piece in pieces for w in (piece, to_core(piece))]

    tied = lax.optimization_barrier
    a, b = 0, 1
    own_a, own_b = pack_pieces(side, own)
    t1a, y0a = along_z(own_a), along_y(own_a)
    t1b = along_z(own_b)
    own_c = to_core(own)
    last_rows, first_rows = pack_rows(volume)
    above, below = passed_along(last_rows, "lenslet", 1), passed_along(first_rows, "lenslet", -1)
    volume, scalars = tied((volume, scalars))
    copies = own_rows(volume)
    t1a, y0a, copies = tied((t1a, y0a, copies))
    t2a, y1a, y0b = along_z(t1a), along_y(t1a), along_x(y0a)
    r0 = both(t1a, y0a)
    copies = edge_rows(above, below, copies)
    acc = add_pieces(scalars, copies, [own, own_c, own, own_c], [(0, 0, None, BOTH), (0, 0, None, BOTH)], None)
    acc = add_pieces(scalars, copies, r0, [(1, 0, a, BOTH), (0, 1, a, BOTH)], acc)
    t2a, y1a, y0b, t1b, acc = tied((t2a, y1a, y0b, t1b, acc))
    t3a, y2a, t2b = along_z(t2a), along_y(t2a), along_x(t2a)
    r1 = both(t2a, y1a, y0b, t1b)
    acc = add_pieces(scalars, copies, r1, [(2, 0, a, BOTH), (1, 1, a, BOTH), (0, 1, b, BOTH), (1, 0, b, BOTH)], acc)
    t3a, y2a, t2b, acc = tied((t3a, y2a, t2b, acc))
    t3b, y3a, y1b = along_z(t2b), along_y(t3a), along_x(y1a)
    r2 = both(t3a, y2a, t2b)
    acc = add_pieces(scalars, copies, r2, [(3, 0, a, BOTH), (2, 1, a, BOTH), (2, 0, b, BOTH)], acc)
    t3b, y3a, y1b, acc = tied((t3b, y3a, y1b, acc))
    y2b, y3b = along_y(t2b), along_x(y3a)
    r3 = both(t3b, y3a, y1b)
    acc = add_pieces(scalars, copies, r3, [(3, 0, b, BOTH), (3, 1, a, BOTH), (1, 1, b, BOTH)], acc)
    y2b, y3b, acc = tied((y2b, y3b, acc))
    r4 = both(y2b, y3b)
    acc = add_pieces(scalars, copies, r4[0::2], [(2, 1, b, MINE), (3, 1, b, MINE)], acc)
    final = (measured, dark_level.reshape(1, pixels))
    plan = [(2, 1, b, THEIRS), (3, 1, b, THEIRS)]
    return tuple(add_pieces(scalars, copies, r4[1::2], plan, acc, final))


def gathered(volume, measured, operator_rows, offset_counts, offset_table, dark_level):
    depths, rows, columns, pixels = volume.shape
    place, start = placements(offset_counts, offset_table)
    weights = gathered_pairs(operator_rows)
    above = passed_along(volume[:, rows - REACH :], "lenslet", 1)
    below = passed_along(volume[:, :REACH], "lenslet", -1)
    copies = shifted_copies(volume, above, below)
    copies = copies.reshape(SHIFTS * depths, rows + 2 * REACH, columns, pixels)
    return tuple(project(copies, weights, place, start, measured, dark_level))


def body(volume, measured, operator_rows, offset_counts, offset_table, dark_level):
    pairs = operator_rows.shape[0] == 2 * operator_rows.shape[1]
    known = lax.axis_size("lenslet") == 16 and lax.axis_size("frames") == 2
    form = exchanged if pairs and known else gathered
    return form(volume, measured, operator_rows, offset_counts, offset_table, dark_level)


def solution(mesh):
    placed = (
        P("frames", "lenslet", None, None),
        P(("frames", "lenslet"), None, None),
        P("lenslet", None),
        P(),
        P(),
        P(),
    )
    return jax.shard_map(
        body,
        mesh=mesh,
        in_specs=placed,
        out_specs=(P(("frames", "lenslet"), None, None), P(("frames", "lenslet"), None, None)),
        check_vma=False,
    )
```

```python
import functools

import jax
import jax.numpy as jnp
from jax import lax
from jax.experimental import pallas as pl
from jax.experimental.pallas import tpu as pltpu
from jax.sharding import PartitionSpec as P

REACH = 2
SHIFTS = 2 * REACH + 1
VMEM = 60 * 1024 * 1024
SMALL = 12 * 1024 * 1024
TILE = 16
LANES = 128
GROUP = 16
EDGE = 32
MINE, THEIRS, BOTH = (0,), (1,), (0, 1)


def passed_along(block, axis, distance):
    devices = range(lax.axis_size(axis))
    route = [(i - distance, i) for i in devices if i - distance in devices]
    return lax.ppermute(block, axis, route)


def shift_kernel(own_ref, above_ref, below_ref, out_ref):
    rows, columns, pixels = own_ref.shape[1:]
    col = lax.broadcasted_iota(jnp.int32, (columns, pixels), 0)

    def put(row, plane):
        wide = plane.astype(jnp.float32)
        for s in range(SHIFTS):
            step = s - REACH
            if step == 0:
                moved = wide
            else:
                moved = pltpu.roll(wide, (-step) % columns, 0)
                inside = col < columns - step if step > 0 else col >= -step
                moved = jnp.where(inside, moved, 0.0)
            out_ref[s, 0, row] = moved.astype(jnp.bfloat16)

    for r in range(REACH):
        put(r, above_ref[0, r])
        put(rows + REACH + r, below_ref[0, r])

    def step(r, carry):
        put(r + REACH, own_ref[0, r])
        return carry

    lax.fori_loop(0, rows, step, 0)


def shifted_copies(volume, above, below):
    depths, rows, columns, pixels = volume.shape
    ext = rows + 2 * REACH
    return pl.pallas_call(
        shift_kernel,
        grid=(depths,),
        in_specs=[
            pl.BlockSpec((1, rows, columns, pixels), lambda d: (d, 0, 0, 0)),
            pl.BlockSpec((1, REACH, columns, pixels), lambda d: (d, 0, 0, 0)),
            pl.BlockSpec((1, REACH, columns, pixels), lambda d: (d, 0, 0, 0)),
        ],
        out_specs=pl.BlockSpec((SHIFTS, 1, ext, columns, pixels), lambda d: (0, d, 0, 0, 0)),
        out_shape=jax.ShapeDtypeStruct((SHIFTS, depths, ext, columns, pixels), jnp.bfloat16),
        compiler_params=pltpu.CompilerParams(vmem_limit_bytes=VMEM),
        name="shifted_copies",
    )(volume, above, below)


def project_kernel(place_ref, start_ref, w_ref, even_ref, odd_ref, meas_ref, dark_ref, pred_ref, ratio_ref):
    i = pl.program_id(0)
    rows, columns, pixels = pred_ref.shape
    dims = (((1,), (1,)), ((), ()))
    a = even_ref[0].reshape(rows * columns, pixels)
    b = odd_ref[0].reshape(rows * columns, pixels)
    w = w_ref[0]
    part = lax.dot_general(a, w[:, :pixels], dims, preferred_element_type=jnp.float32)
    part = part + lax.dot_general(b, w[:, pixels:], dims, preferred_element_type=jnp.float32)
    part = part.reshape(rows, columns, pixels)

    @pl.when(i == 0)
    def _():
        pred_ref[...] = part

    @pl.when(i > 0)
    def _():
        pred_ref[...] = pred_ref[...] + part

    @pl.when(i == pl.num_programs(0) - 1)
    def _():
        ratio_ref[...] = meas_ref[...] / (pred_ref[...] + dark_ref[...])


def project(copies, weights, place, start, measured, dark_level):
    rows, columns, pixels = measured.shape
    shards, _, pair = weights.shape
    whole = lambda i, *_: (0, 0, 0)

    def slab(which):
        return pl.BlockSpec(
            (pl.Element(1), pl.Element(rows), pl.Element(columns), pl.Element(pixels)),
            lambda i, place_ref, start_ref: (
                place_ref[jnp.minimum(2 * i + which, 2 * shards - 1)],
                start_ref[jnp.minimum(2 * i + which, 2 * shards - 1)],
                0,
                0,
            ),
        )

    grid_spec = pltpu.PrefetchScalarGridSpec(
        num_scalar_prefetch=2,
        grid=(shards,),
        in_specs=[
            pl.BlockSpec((1, pixels, pair), lambda i, *_: (i, 0, 0)),
            slab(0),
            slab(1),
            pl.BlockSpec((rows, columns, pixels), whole),
            pl.BlockSpec((1, 1, pixels), whole),
        ],
        out_specs=[pl.BlockSpec((rows, columns, pixels), whole)] * 2,
    )
    return pl.pallas_call(
        project_kernel,
        grid_spec=grid_spec,
        out_shape=[jax.ShapeDtypeStruct(measured.shape, jnp.float32)] * 2,
        compiler_params=pltpu.CompilerParams(vmem_limit_bytes=VMEM),
        name="project",
    )(place, start, weights, copies, copies, measured, dark_level.reshape(1, 1, pixels))


def gathered_pairs(operator_rows):
    held, pixels = operator_rows.shape
    if held == 2 * pixels:
        return lax.all_gather(operator_rows.T, "lenslet", axis=0)
    every = lax.all_gather(operator_rows, "lenslet", axis=0, tiled=True)
    return every.reshape(-1, 2 * pixels, pixels).transpose(0, 2, 1)


IN_VMEM = pl.BlockSpec(memory_space=pltpu.VMEM)
IN_SMEM = pl.BlockSpec(memory_space=pltpu.SMEM)
IN_HBM = pl.BlockSpec(memory_space=pl.ANY)


def put_shifted(out_ref, depth, row, plane):
    columns, pixels = plane.shape
    wide = plane.astype(jnp.float32)
    col = lax.broadcasted_iota(jnp.int32, (columns, pixels), 0)
    depths = out_ref.shape[0] // SHIFTS
    for s in range(SHIFTS):
        step = s - REACH
        if step == 0:
            out_ref[s * depths + depth, row] = plane
            continue
        moved = pltpu.roll(wide, (-step) % columns, 0)
        inside = col < columns - step if step > 0 else col >= -step
        out_ref[s * depths + depth, row] = jnp.where(inside, moved, 0.0).astype(jnp.bfloat16)


def own_rows_kernel(volume_ref, out_ref, held, sems):
    depths, rows, _, _ = held.shape
    fetch = [pltpu.make_async_copy(volume_ref.at[d], held.at[d], sems.at[d]) for d in range(depths)]
    for copy in fetch:
        copy.start()
    for d, copy in enumerate(fetch):
        copy.wait()

        def step(r, carry, d=d):
            put_shifted(out_ref, d, r + REACH, held[d, r])
            return carry

        lax.fori_loop(0, rows, step, 0)


def edge_rows_kernel(above_ref, below_ref, old_ref, out_ref):
    depths = out_ref.shape[0] // SHIFTS
    rows, columns, pixels = out_ref.shape[1] - 2 * REACH, out_ref.shape[2], out_ref.shape[3]
    tail = pixels - above_ref.shape[1]
    pieces = columns // EDGE
    for k in range(depths * REACH):
        for packed, begin in ((above_ref, 0), (below_ref, rows + REACH)):
            left = [packed[:EDGE, tail * (k * pieces + j) : tail * (k * pieces + j + 1)] for j in range(pieces)]
            plane = packed[EDGE + k * columns : EDGE + (k + 1) * columns]
            plane = jnp.concatenate([plane, jnp.concatenate(left, axis=0)], axis=1)
            put_shifted(out_ref, k // REACH, begin + k % REACH, plane)


def own_rows(volume):
    depths, rows, columns, pixels = volume.shape
    shape = (SHIFTS * depths, rows + 2 * REACH, columns, pixels)
    return pl.pallas_call(
        own_rows_kernel,
        in_specs=[pl.BlockSpec(memory_space=pltpu.HBM)],
        scratch_shapes=[pltpu.VMEM(volume.shape, volume.dtype), pltpu.SemaphoreType.DMA((depths,))],
        out_specs=IN_VMEM,
        out_shape=pltpu.VMEM(shape, volume.dtype),
        compiler_params=pltpu.CompilerParams(vmem_limit_bytes=SMALL),
        name="own_rows",
    )(pltpu.with_memory_space_constraint(volume, pltpu.HBM))


def edge_rows(above, below, copies):
    return pl.pallas_call(
        edge_rows_kernel,
        in_specs=[IN_VMEM, IN_VMEM, IN_VMEM],
        out_specs=IN_VMEM,
        out_shape=pltpu.VMEM(copies.shape, copies.dtype),
        input_output_aliases={2: 0},
        compiler_params=pltpu.CompilerParams(vmem_limit_bytes=SMALL),
        name="edge_rows",
    )(above, below, copies)


def pack_pieces_kernel(side_ref, own_ref, a_ref, b_ref):
    _, part, pair = own_ref.shape
    pixels = pair // 2
    wide = pixels // LANES * LANES
    side = side_ref[0]
    for out_ref, half in ((a_ref, side), (b_ref, 1 - side)):
        w = own_ref[half]
        out_ref[GROUP:, :wide] = w[:, :wide]
        out_ref[GROUP:, wide:] = w[:, pixels : pixels + wide]
        left = jnp.concatenate([w[:, wide:pixels], w[:, pixels + wide :]], axis=1)
        tail = left.shape[1]
        groups = -(-part // GROUP)
        left = jnp.concatenate([left, jnp.zeros((groups * GROUP - part, tail), left.dtype)], axis=0)
        cut = [left[GROUP * n : GROUP * (n + 1)] for n in range(groups)]
        cut.append(jnp.zeros((GROUP, 2 * wide - groups * tail), left.dtype))
        out_ref[:GROUP] = jnp.concatenate(cut, axis=1)


def pack_pieces(side, own):
    _, part, pair = own.shape
    packed = jax.ShapeDtypeStruct((GROUP + part, pair // 2 // LANES * LANES * 2), own.dtype)
    return pl.pallas_call(
        pack_pieces_kernel,
        in_specs=[IN_SMEM, IN_VMEM],
        out_specs=[IN_VMEM] * 2,
        out_shape=[pltpu.VMEM(packed.shape, packed.dtype)] * 2,
        compiler_params=pltpu.CompilerParams(vmem_limit_bytes=SMALL),
        name="pack_pieces",
    )(side.reshape(1), own)


def unpacked(w_ref, n, which, part, pixels):
    if len(w_ref.shape) == 3:
        return w_ref[n, :, pixels * which : pixels * (which + 1)]
    wide = w_ref.shape[1] // 2
    tail = pixels - wide
    groups = -(-part // GROUP)
    first = [w_ref[:GROUP, 2 * tail * k + tail * which : 2 * tail * k + tail * (which + 1)] for k in range(groups)]
    left = jnp.concatenate(first, axis=0)[:part]
    return jnp.concatenate([w_ref[GROUP:, wide * which : wide * (which + 1)], left], axis=1)


def pack_rows_kernel(volume_ref, last_ref, first_ref, held, sems):
    depths, rows, columns, pixels = volume_ref.shape
    wide = pixels // LANES * LANES
    begins = (rows - REACH, 0)
    fetch = [
        pltpu.make_async_copy(volume_ref.at[:, pl.ds(begin, REACH)], held.at[n], sems.at[n])
        for n, begin in enumerate(begins)
    ]
    for copy in fetch:
        copy.start()
    for n, out_ref in enumerate((last_ref, first_ref)):
        fetch[n].wait()
        cut = []
        for k in range(depths * REACH):
            plane = held[n, k // REACH, k % REACH]
            out_ref[EDGE + k * columns : EDGE + (k + 1) * columns] = plane[:, :wide]
            cut += [plane[EDGE * j : EDGE * (j + 1), wide:] for j in range(columns // EDGE)]
        cut.append(jnp.zeros((EDGE, wide - len(cut) * (pixels - wide)), volume_ref.dtype))
        out_ref[:EDGE] = jnp.concatenate(cut, axis=1)


def pack_rows(volume):
    depths, _, columns, pixels = volume.shape
    shape = (EDGE + depths * REACH * columns, pixels // LANES * LANES)
    return pl.pallas_call(
        pack_rows_kernel,
        in_specs=[pl.BlockSpec(memory_space=pltpu.HBM)],
        out_specs=[IN_VMEM] * 2,
        out_shape=[pltpu.VMEM(shape, volume.dtype)] * 2,
        scratch_shapes=[
            pltpu.VMEM((2, depths, REACH, columns, pixels), volume.dtype),
            pltpu.SemaphoreType.DMA((2,)),
        ],
        compiler_params=pltpu.CompilerParams(vmem_limit_bytes=SMALL),
        name="pack_rows",
    )(pltpu.with_memory_space_constraint(volume, pltpu.HBM))


def operator_spot(scalars, op, depths):
    end, depth = jnp.int32(0), jnp.int32(0)
    for d in range(depths):
        end = end + scalars[d]
        depth = depth + jnp.where(op >= end, 1, 0)
    at = depths + 2 * op
    return (scalars[at + 1] + REACH) * depths + depth, scalars[at] + REACH


def add_kernel(scalars, copies, *refs, plan, pieces, first, last):
    weights = refs[:pieces]
    refs = refs[pieces:]
    if last:
        meas, dark, old, pred_out, ratio_out, acc, pred, ratio, sems = refs
    elif first:
        old, acc = None, refs[0]
    else:
        old, acc = refs
    depths = copies.shape[0] // SHIFTS
    columns, pixels = copies.shape[2:]
    lines = acc.shape[1]
    rows = lines // columns
    here, side = scalars[scalars.shape[0] - 2], scalars[scalars.shape[0] - 1]
    dims = (((1,), (1,)), ((), ()))
    jobs, at = [], 0
    for n, (hops, other, kind, cores) in enumerate(plan):
        shard = ((here + (16 - 4 * hops)) % 16) ^ (2 * other)
        half = n if kind is None else side ^ kind
        products = []
        for core in cores:
            for which in range(2):
                copy, row = operator_spot(scalars, 2 * (shard ^ core) + which, depths)
                products.append((at, which, copy, row))
            at += 1
        jobs.append((n, half, products))

    tile = 4 if last else TILE
    for t in range(rows // tile):
        m = slice(t * tile * columns, (t + 1) * tile * columns)
        for n, half, products in jobs:
            total = None
            for at, which, copy, row in products:
                w = unpacked(weights[at], n, which, acc.shape[2], pixels)
                slab = copies[copy, pl.ds(row + t * tile, tile)].reshape(tile * columns, pixels)
                part = lax.dot_general(slab, w, dims, preferred_element_type=jnp.float32)
                total = part if total is None else total + part
            if first:
                acc[half, m] = total
            elif last and n == 0:
                acc[half, m] = old[half, m] + total
                acc[1 - half, m] = old[1 - half, m]
            elif last:
                acc[half, m] = acc[half, m] + total
            else:
                acc[half, m] = acc[half, m] + total if n else old[half, m] + total
        if last:
            r = slice(t * tile, (t + 1) * tile)
            full = jnp.concatenate([acc[0, m], acc[1, m]], axis=1).reshape(tile, columns, pixels)
            pred[r] = full
            ratio[r] = meas[r] / (full + dark[...].reshape(1, 1, pixels))
            for q, (src, dst) in enumerate(((pred, pred_out), (ratio, ratio_out))):
                pltpu.make_async_copy(src.at[r], dst.at[r], sems.at[2 * t + q]).start()
    if last:
        for t in range(rows // tile):
            r = slice(t * tile, (t + 1) * tile)
            for q, (src, dst) in enumerate(((pred, pred_out), (ratio, ratio_out))):
                pltpu.make_async_copy(src.at[r], dst.at[r], sems.at[2 * t + q]).wait()


def add_pieces(scalars, copies, weights, plan, acc, final=None):
    columns, pixels = copies.shape[2:]
    rows = copies.shape[1] - 2 * REACH
    lines, part = rows * columns, pixels // 2
    pieces = len(weights)
    operands = [scalars, copies, *weights]
    shape = (2, lines, part)
    scratch, params = [], {}
    alias = {}
    if final is not None:
        operands += [*final, acc]
        full = final[0].shape
        out_shape = [jax.ShapeDtypeStruct(full, jnp.float32)] * 2
        out_specs = [IN_HBM] * 2
        scratch = [pltpu.VMEM(shape, jnp.float32), pltpu.VMEM(full, jnp.float32), pltpu.VMEM(full, jnp.float32)]
        scratch.append(pltpu.SemaphoreType.DMA((2 * (rows // 4),)))
    else:
        out_shape, out_specs = pltpu.VMEM(shape, jnp.float32), IN_VMEM
        if acc is not None:
            alias = {len(operands): 0}
            operands.append(acc)
    flops = 2 * lines * 4 * pixels * part * pieces
    return pl.pallas_call(
        functools.partial(add_kernel, plan=plan, pieces=pieces, first=acc is None, last=final is not None),
        in_specs=[IN_SMEM] + [IN_VMEM] * (len(operands) - 1),
        out_specs=out_specs,
        out_shape=out_shape,
        scratch_shapes=scratch,
        input_output_aliases=alias,
        cost_estimate=pl.CostEstimate(flops=flops, bytes_accessed=pieces * 1024 * 1024, transcendentals=0),
        compiler_params=pltpu.CompilerParams(vmem_limit_bytes=SMALL),
        name="add_pieces",
    )(*operands)


def placements(offset_counts, offset_table):
    depths = offset_counts.shape[0]
    planes = jnp.arange(depths, dtype=jnp.int32)
    ends = jnp.sum(jnp.where(planes[None, :] <= planes[:, None], offset_counts[None, :], 0), axis=1)
    positions = jnp.arange(offset_table.shape[0], dtype=jnp.int32)
    depth_of = jnp.sum((positions[:, None] >= ends[None, :]).astype(jnp.int32), axis=1)
    return (offset_table[:, 1] + REACH) * depths + depth_of, offset_table[:, 0] + REACH


def exchanged(volume, measured, operator_rows, offset_counts, offset_table, dark_level):
    depths, rows, columns, pixels = volume.shape
    part = pixels // 2
    side = lax.axis_index("frames")
    here = lax.axis_index("lenslet")
    count = lax.axis_size("lenslet")
    scalars = jnp.concatenate([offset_counts, offset_table.reshape(-1), jnp.stack([here, side])])

    up = [(i, (i + 4) % count) for i in range(count)]
    beside = [(i, i ^ 2) for i in range(count)]
    twin = [(i, i ^ 1) for i in range(count)]
    along_z = lambda v: lax.ppermute(v, "lenslet", up)
    along_y = lambda v: lax.ppermute(v, "lenslet", beside)
    to_core = lambda v: lax.ppermute(v, "lenslet", twin)
    along_x = lambda v: lax.ppermute(v, "frames", [(0, 1), (1, 0)])

    own = operator_rows.T.reshape(2, part, 2 * pixels)
    both = lambda *pieces: [w for piece in pieces for w in (piece, to_core(piece))]

    tied = lax.optimization_barrier
    a, b = 0, 1
    own_a, own_b = pack_pieces(side, own)
    t1a, y0a = along_z(own_a), along_y(own_a)
    t1b = along_z(own_b)
    own_c = to_core(own)
    last_rows, first_rows = pack_rows(volume)
    above, below = passed_along(last_rows, "lenslet", 1), passed_along(first_rows, "lenslet", -1)
    volume, scalars = tied((volume, scalars))
    copies = own_rows(volume)
    t1a, y0a, copies = tied((t1a, y0a, copies))
    t2a, y1a, y0b = along_z(t1a), along_y(t1a), along_x(y0a)
    r0 = both(t1a, y0a)
    copies = edge_rows(above, below, copies)
    acc = add_pieces(scalars, copies, [own, own_c, own, own_c], [(0, 0, None, BOTH), (0, 0, None, BOTH)], None)
    acc = add_pieces(scalars, copies, r0, [(1, 0, a, BOTH), (0, 1, a, BOTH)], acc)
    t2a, y1a, y0b, t1b, acc = tied((t2a, y1a, y0b, t1b, acc))
    t3a, y2a, t2b = along_z(t2a), along_y(t2a), along_x(t2a)
    r1 = both(t2a, y1a, y0b, t1b)
    acc = add_pieces(scalars, copies, r1, [(2, 0, a, BOTH), (1, 1, a, BOTH), (0, 1, b, BOTH), (1, 0, b, BOTH)], acc)
    t3a, y2a, t2b, acc = tied((t3a, y2a, t2b, acc))
    t3b, y3a, y1b = along_z(t2b), along_y(t3a), along_x(y1a)
    r2 = both(t3a, y2a, t2b)
    acc = add_pieces(scalars, copies, r2, [(3, 0, a, BOTH), (2, 1, a, BOTH), (2, 0, b, BOTH)], acc)
    t3b, y3a, y1b, acc = tied((t3b, y3a, y1b, acc))
    y2b, y3b = along_y(t2b), along_x(y3a)
    r3 = both(t3b, y3a, y1b)
    acc = add_pieces(scalars, copies, r3, [(3, 0, b, BOTH), (3, 1, a, BOTH), (1, 1, b, BOTH)], acc)
    y2b, y3b, acc = tied((y2b, y3b, acc))
    r4 = both(y2b, y3b)
    acc = add_pieces(scalars, copies, r4[0::2], [(2, 1, b, MINE), (3, 1, b, MINE)], acc)
    final = (measured, dark_level.reshape(1, pixels))
    plan = [(2, 1, b, THEIRS), (3, 1, b, THEIRS)]
    return tuple(add_pieces(scalars, copies, r4[1::2], plan, acc, final))


def gathered(volume, measured, operator_rows, offset_counts, offset_table, dark_level):
    depths, rows, columns, pixels = volume.shape
    place, start = placements(offset_counts, offset_table)
    weights = gathered_pairs(operator_rows)
    above = passed_along(volume[:, rows - REACH :], "lenslet", 1)
    below = passed_along(volume[:, :REACH], "lenslet", -1)
    copies = shifted_copies(volume, above, below)
    copies = copies.reshape(SHIFTS * depths, rows + 2 * REACH, columns, pixels)
    return tuple(project(copies, weights, place, start, measured, dark_level))


def body(volume, measured, operator_rows, offset_counts, offset_table, dark_level):
    pairs = operator_rows.shape[0] == 2 * operator_rows.shape[1]
    known = lax.axis_size("lenslet") == 16 and lax.axis_size("frames") == 2
    form = exchanged if pairs and known else gathered
    return form(volume, measured, operator_rows, offset_counts, offset_table, dark_level)


def solution(mesh):
    placed = (
        P("frames", "lenslet", None, None),
        P(("frames", "lenslet"), None, None),
        P("lenslet", None),
        P(),
        P(),
        P(),
    )
    return jax.shard_map(
        body,
        mesh=mesh,
        in_specs=placed,
        out_specs=(P(("frames", "lenslet"), None, None), P(("frames", "lenslet"), None, None)),
        check_vma=False,
    )
```
